512 devices in a mesh: blk: 128 (over z, y, x_lo), rep: 4 (over x_hi, core).
Axes of the slice: x: 4 (x_hi: 2, x_lo: 2; x = x_hi * 2 + x_lo), y: 8, z: 8, core: 2. Of those that a mesh axis runs over, the one named last changes fastest.
Arguments:
- left_emb: float32 [32768, 256], P('blk'), may hold values from -6 to 6
- left_state: float32 [32768], P('blk'), may hold values from 0.3 to 30
- right_emb: float32 [32768, 256], P('blk'), may hold values from -8 to 8
- right_state: float32 [32768], P('blk'), may hold values from 0.3 to 30
- relation: float32 [2, 256, 256], replicated, may hold values from -0.375 to 0.375
- relation_state: float32 [2, 256, 256], replicated, may hold values from 5242.88 to 524288
- edge_src: int32 [128, 4, 2, 2, 512], P('blk', 'rep'), may hold values from 0 to 255
- edge_dst: int32 [128, 4, 2, 2, 512], P('blk', 'rep'), may hold values from 0 to 255
- edge_rel: int32 [128, 4, 2, 2, 512], P('blk', 'rep'), may hold values from 0 to 1
- negatives: int32 [128, 4, 2, 2, 512], P('blk', 'rep'), may hold values from 0 to 255
- batch_counts: int32 [128, 4, 2], P('blk', 'rep'), may hold values from 0 to 2, as said below
Outputs:
- left_new: float32 [32768, 256], P('blk')
- left_state_new: float32 [32768], P('blk')
- right_new: float32 [32768, 256], P('blk')
- right_state_new: float32 [32768], P('blk')
- relation_new: float32 [2, 256, 256], replicated
- relation_state_new: float32 [2, 256, 256], replicated
The draws below stay inside these ranges and needn't reach their ends.
Inputs may be any that keep to these rules, and one draw needn't show every extreme that they name: `batch_counts`: in each bucket the live edge batches of the 4 devices of one blk index number at most 4; in every draw some bucket has exactly that many, with some device at 2.
All inputs are finite; a program needn't handle non-finite values.
Results may differ from the reference program's by a relative error of at most 0.035.
Values sent between devices are 32-bit elements; how exact they have to be, the bound alone decides.
No kernel may reach another device: no remote copies, remote signals or barrier semaphores. Data moves between devices by JAX's collectives and lax.ppermute only.
A program may use at most 64 MiB of HBM per device.

```python
import math
import jax
import jax.numpy as jnp
from jax import lax

D = 256
NEG = 512
NREL = 2
ROWS = 256
BATCH = 512
NBATCH = 2
REPS = 4
BLOCKS = 128


def draw_right_emb(key, part):
    first_key, second_key = jax.random.split(jax.random.fold_in(key, 11))
    values = jnp.clip(jax.random.normal(first_key, (BLOCKS * ROWS, D), jnp.float32), -4.0, 4.0)
    row_scale = jnp.exp(jax.random.uniform(second_key, (BLOCKS * ROWS, 1), jnp.float32, jnp.log(0.5), jnp.log(2.0)))
    return (values * row_scale).astype(jnp.float32)


def draw_batch_counts(key, part):
    first_key, second_key, third_key = jax.random.split(jax.random.fold_in(key, 23), 3)
    raw_counts = jax.random.randint(first_key, (BLOCKS * 2, REPS), 0, NBATCH + 1)
    limit_total = REPS * (NBATCH // 2)
    taken = jnp.zeros((BLOCKS * 2,), jnp.int32)
    columns = []
    for member in range(REPS):
        column = jnp.minimum(raw_counts[:, member], limit_total - taken)
        taken = taken + column
        columns.append(column)
    flattened = jnp.stack(columns, axis=1)
    chosen = jax.random.randint(second_key, (), 0, BLOCKS * 2)
    offset = jax.random.randint(third_key, (), 0, REPS)
    pattern = jnp.where((jnp.arange(REPS) - offset) % REPS < REPS // 2, NBATCH, 0).astype(jnp.int32)
    flattened = jnp.where((jnp.arange(BLOCKS * 2) == chosen)[:, None], pattern[None, :], flattened)
    return flattened.reshape(BLOCKS, 2, REPS).transpose(0, 2, 1).astype(jnp.int32)


def place_ends(array, rng, low, high):
    dims = array.shape
    place = [jax.random.randint(jax.random.fold_in(rng, axis), (), 0, dims[axis]) for axis in range(len(dims))]
    array = array.at[tuple(place)].set(low)
    longest = dims.index(max(dims))
    place[longest] = (place[longest] + 1) % dims[longest]
    return array.at[tuple(place)].set(high)


def block_scale(rng, shape, cuts, smallest, top_value):
    def one(dim, shards_of):
        steps = jax.random.uniform(jax.random.fold_in(jax.random.fold_in(rng, 6), dim), (shards_of,), jnp.float32, smallest / len(cuts), top_value / len(cuts))
        return jnp.repeat(jnp.exp(steps), shape[dim] // shards_of).reshape((-1,) + (1,) * (len(shape) - dim - 1))

    level = one(*cuts[0])
    for cut in cuts[1:]:
        level = level * one(*cut)
    return level


def normal_values(key, shape, deviation, most, pieces=(), dtype=jnp.bfloat16):
    factor_of = block_scale(key, shape, pieces, -0.22, 0.18) if pieces else 1.0
    result = jax.random.normal(key, shape, jnp.float32) * deviation * factor_of
    return jnp.minimum(jnp.maximum(result, -most), most).astype(dtype)


def setup_inputs(seed: int = 0) -> dict:
    keys = jax.random.split(jax.random.key(seed), 12)
    return {
        "left_emb": normal_values(keys[0], (BLOCKS * ROWS, D), 1.0, 6.0, ((0, 128),), jnp.float32),
        "left_state": jnp.clip(jnp.exp(math.log(30.0) - 4.6051701 * jax.random.uniform(keys[1], (BLOCKS * ROWS,), jnp.float32) ** block_scale(keys[1], (BLOCKS * ROWS,), ((0, 128),), -0.2, 0.2)), 0.3, 30.0),
        "right_emb": draw_right_emb(jax.random.fold_in(keys[11], 71), 0),
        "right_state": jnp.clip(jnp.exp(math.log(30.0) - 4.6051701 * jax.random.uniform(keys[3], (BLOCKS * ROWS,), jnp.float32) ** block_scale(keys[3], (BLOCKS * ROWS,), ((0, 128),), -0.2, 0.2)), 0.3, 30.0),
        "relation": normal_values(keys[4], (NREL, D, D), D ** -0.5, 0.375, (), jnp.float32),
        "relation_state": jnp.clip(jnp.exp(jax.random.uniform(keys[5], (NREL, D, D), jnp.float32, math.log(5242.88), math.log(524288.0))), 5242.88, 524288.0),
        "edge_src": place_ends(jax.random.randint(keys[6], (BLOCKS, REPS, 2, NBATCH, BATCH), 0, ROWS), jax.random.fold_in(keys[6], 1), 0, ROWS - 1).astype(jnp.int32),
        "edge_dst": place_ends(jax.random.randint(keys[7], (BLOCKS, REPS, 2, NBATCH, BATCH), 0, ROWS), jax.random.fold_in(keys[7], 1), 0, ROWS - 1).astype(jnp.int32),
        "edge_rel": place_ends(jax.random.randint(keys[8], (BLOCKS, REPS, 2, NBATCH, BATCH), 0, NREL), jax.random.fold_in(keys[8], 1), 0, NREL - 1).astype(jnp.int32),
        "negatives": place_ends(jax.random.randint(keys[9], (BLOCKS, REPS, 2, NBATCH, NEG), 0, ROWS), jax.random.fold_in(keys[9], 1), 0, ROWS - 1).astype(jnp.int32),
        "batch_counts": draw_batch_counts(jax.random.fold_in(keys[11], 71), 0),
    }


learn_rate = 0.1

def batch_terms(query_table, right_bf, src_row, dst_row, rel_row, neg_row, live_flag):
    queries = query_table[rel_row, src_row]
    pos_rows = right_bf[dst_row]
    neg_rows = right_bf[neg_row]
    pos_score = lax.optimization_barrier(jnp.sum(queries.astype(jnp.float32) * pos_rows.astype(jnp.float32), axis=-1))
    neg_score = lax.dot_general(queries, neg_rows, (((1,), (1,)), ((), ())), preferred_element_type=jnp.float32)
    row_top = jnp.maximum(lax.optimization_barrier(jnp.max(neg_score, axis=1)), pos_score)
    pos_exp = jnp.exp(pos_score - row_top)
    neg_exp = jnp.exp(neg_score - row_top[:, None])
    row_total = pos_exp + lax.optimization_barrier(jnp.sum(neg_exp, axis=1))
    pos_weight = (pos_exp / row_total - 1.0) * live_flag
    weights = (neg_exp / row_total[:, None] * live_flag).astype(jnp.bfloat16)
    query_grad = jnp.dot(weights, neg_rows, preferred_element_type=jnp.float32) + pos_weight[:, None] * pos_rows.astype(jnp.float32)
    neg_grad = lax.dot_general(weights, queries, (((0,), (0,)), ((), ())), preferred_element_type=jnp.float32)
    pos_grad = pos_weight[:, None] * queries.astype(jnp.float32)
    return (query_grad, neg_grad, pos_grad)

def device_terms(query_table, right_bf, sources, targets, relations, negs, live_count):
    nrel, rows, width = query_table.shape

    def step(position, carry):
        table_grad, right_grad = carry
        live_flag = (position < live_count).astype(jnp.float32)
        src_row = sources[position]
        dst_row = targets[position]
        rel_row = relations[position]
        neg_row = negs[position]
        query_grad, neg_grad, pos_grad = batch_terms(query_table, right_bf, src_row, dst_row, rel_row, neg_row, live_flag)
        table_grad = table_grad.at[rel_row, src_row].add(query_grad)
        right_grad = right_grad.at[neg_row].add(neg_grad).at[dst_row].add(pos_grad)
        return (table_grad, right_grad)
    start = (jnp.zeros((nrel, rows, width), jnp.float32), jnp.zeros((rows, width), jnp.float32))
    return lax.fori_loop(0, sources.shape[0], step, start)

def row_update(embedding, accum, gradient):
    accum_next = accum + lax.optimization_barrier(jnp.mean(gradient * gradient, axis=-1))
    return (embedding - learn_rate * gradient / jnp.sqrt(accum_next)[..., None], accum_next)

def reference(left_emb, left_state, right_emb, right_state, relation, relation_state, edge_src, edge_dst, edge_rel, negatives, batch_counts):
    left_blocks = left_emb.reshape(BLOCKS, ROWS, D)
    left_accum = left_state.reshape(BLOCKS, ROWS)
    right_blocks = right_emb.reshape(BLOCKS, ROWS, D)
    right_accum = right_state.reshape(BLOCKS, ROWS)
    operator_bf = relation.astype(jnp.bfloat16)
    operator_total = jnp.zeros((NREL, D, D), jnp.float32)
    for bucket in range(2):

        def per_block(carry, inputs):
            left_rows, right_rows, sources, targets, relations, negs, counts = inputs
            left_bf = left_rows.astype(jnp.bfloat16)
            right_bf = right_rows.astype(jnp.bfloat16)
            query_table = jnp.einsum('nd,rkd->rnk', left_bf.astype(jnp.float32), operator_bf.astype(jnp.float32)).astype(jnp.bfloat16)
            left_grad = jnp.zeros((ROWS, D), jnp.float32)
            right_grad = jnp.zeros((ROWS, D), jnp.float32)
            operator_grad = jnp.zeros((NREL, D, D), jnp.float32)
            for member in range(REPS):
                table_grad, member_right = device_terms(query_table, right_bf, sources[member, bucket], targets[member, bucket], relations[member, bucket], negs[member, bucket], counts[member, bucket])
                table_bf = table_grad.astype(jnp.bfloat16)
                left_grad = left_grad + jnp.einsum('rnk,rkd->nd', table_bf.astype(jnp.float32), operator_bf.astype(jnp.float32))
                operator_grad = operator_grad + jnp.einsum('rnk,nd->rkd', table_bf.astype(jnp.float32), left_bf.astype(jnp.float32))
                right_grad = right_grad + member_right
            return (carry + operator_grad, (left_grad, right_grad))
        operator_total, (left_grads, right_grads) = lax.scan(per_block, operator_total, (left_blocks, right_blocks, edge_src, edge_dst, edge_rel, negatives, batch_counts))
        left_blocks, left_accum = row_update(left_blocks, left_accum, left_grads)
        right_blocks, right_accum = row_update(right_blocks, right_accum, right_grads)
        if bucket == 0:
            left_blocks = jnp.roll(left_blocks, 1, axis=0)
            left_accum = jnp.roll(left_accum, 1, axis=0)
    relation_state_new = relation_state + operator_total * operator_total
    relation_new = relation - learn_rate * operator_total / jnp.sqrt(relation_state_new)
    return (left_blocks.reshape(BLOCKS * ROWS, D), left_accum.reshape(BLOCKS * ROWS), right_blocks.reshape(BLOCKS * ROWS, D), right_accum.reshape(BLOCKS * ROWS), relation_new, relation_state_new)
```

```python
import functools

import jax
import jax.numpy as jnp
from jax import lax
from jax.experimental import pallas as pl
from jax.experimental.pallas import tpu as pltpu
from jax.sharding import PartitionSpec as P

learn_rate = 0.1
BF = jnp.bfloat16
F32 = jnp.float32


def dot(a, b, dims):
    return lax.dot_general(a, b, ((dims[:1], dims[1:]), ((), ())), preferred_element_type=F32)


def same(rows, cols):
    shape = (rows, cols)
    return lax.broadcasted_iota(jnp.int32, shape, 0) == lax.broadcasted_iota(jnp.int32, shape, 1)


def to_column(row):
    size = row.shape[1]
    return jnp.sum(jnp.where(same(size, size), row, 0.0), axis=1, keepdims=True)


def to_row(column):
    size = column.shape[0]
    return jnp.sum(jnp.where(same(size, size), column, 0.0), axis=0, keepdims=True)


def one_hot(index_row, count):
    rows = lax.broadcasted_iota(jnp.int32, (count, index_row.shape[1]), 0)
    return jnp.where(rows == index_row, 1.0, 0.0).astype(BF)


def row_update(embedding, accum_row, gradient):
    mean = jnp.mean(gradient * gradient, axis=1, keepdims=True)
    accum = to_column(accum_row) + mean
    return embedding - learn_rate * gradient / jnp.sqrt(accum), to_row(accum)


def bucket_kernel(
    bucket, nbatch, idx_ref, left_ref, accum_ref, right_ref, right_accum_ref, op_ref, *refs
):
    if bucket == 0:
        left_out, right_out, right_accum_out, grad_out = refs[:4]
    else:
        grad_in, left_out, left_accum_out, right_out, right_accum_out, grad_out = refs[:6]
    query_t, scores_t, total, table_t = refs[-4:]
    nrel, width, _ = op_ref.shape
    rows = right_ref.shape[0]
    pairs = nrel * rows
    left = left_ref[0:rows, :]
    left_bf = left.astype(BF)
    right = right_ref[...]
    right_bf = right.astype(BF)
    for r in range(nrel):
        query_t[:, r * rows : (r + 1) * rows] = dot(op_ref[r].astype(BF), left_bf, (1, 1)).astype(BF)
    scores_t[...] = dot(right_bf, query_t[...], (1, 0))
    total[...] = jnp.zeros_like(total)

    def member_step(member, _):
        live = jnp.max(idx_ref[member, pl.ds(8 * nbatch + bucket, 1), :])

        def batch_step(batch, _):
            base = (bucket * nbatch + batch) * 4
            source = idx_ref[member, pl.ds(base, 1), :]
            target = idx_ref[member, pl.ds(base + 1, 1), :]
            relation = idx_ref[member, pl.ds(base + 2, 1), :]
            negative = idx_ref[member, pl.ds(base + 3, 1), :]
            edges = dot(one_hot(target, rows), one_hot(relation * rows + source, pairs), (1, 1))
            counts = dot(
                one_hot(negative, rows), jnp.ones((negative.shape[1], 128), BF), (1, 0)
            )
            for start in range(0, pairs, 128):
                cols = slice(start, start + 128)
                score = scores_t[:, cols]
                edge = edges[:, cols]
                top = jnp.max(jnp.where(counts > 0.0, score, -3.0e38), axis=0, keepdims=True)
                above = score - top
                small = jnp.exp(-jnp.abs(above))
                weighted = counts * small
                neg_total = jnp.sum(weighted, axis=0, keepdims=True)
                neg_scale = jnp.where(above > 0.0, small, 1.0)
                pos_exp = jnp.where(above > 0.0, 1.0, small)
                factor = edge * neg_scale / (pos_exp + neg_total * neg_scale)
                factor_sum = jnp.sum(factor, axis=0, keepdims=True)
                total[:, cols] += weighted * factor_sum - neg_total * factor
            return 0

        return lax.fori_loop(0, live, batch_step, 0)

    lax.fori_loop(0, idx_ref.shape[0], member_step, 0)

    total_bf = total[...].astype(BF)
    right_grad = dot(total_bf, query_t[...], (1, 1))
    table_t[...] = dot(right_bf, total_bf, (0, 0)).astype(BF)
    left_grad = jnp.zeros((rows, width), F32)
    for r in range(nrel):
        left_grad += dot(table_t[:, r * rows : (r + 1) * rows], op_ref[r].astype(BF), (0, 0))
    core = lax.axis_index("core")
    mine = table_t[:, pl.ds(pl.multiple_of(core * rows, rows), rows)]
    grad = dot(mine, left_bf, (1, 0))
    if bucket == 0:
        grad_out[...] = grad
        new_left, new_accum = row_update(left, accum_ref[...], left_grad)
        left_out[0:rows, :] = new_left
        left_out[rows : rows + 8, :] = jnp.broadcast_to(new_accum, (8, rows))
    else:
        grad = grad + grad_in[...]
        for half in range(2):
            grad_out[half] = grad[:, half * 128 : (half + 1) * 128].reshape(grad_out.shape[1:])
        accum = accum_ref[rows : rows + 1, :]
        left_out[...], left_accum_out[...] = row_update(left, accum, left_grad)
    right_out[...], right_accum_out[...] = row_update(right, right_accum_ref[...], right_grad)


def run_bucket(bucket, nbatch, idx, left, accum, right, right_accum, relation, grad=None):
    nrel, width, _ = relation.shape
    rows = right.shape[0]
    f32 = lambda *shape: jax.ShapeDtypeStruct(shape, F32)
    if bucket == 0:
        outs = (f32(rows + 8, width), f32(rows, width), f32(1, rows), f32(width, width))
        args = (idx, left, accum, right, right_accum, relation)
    else:
        outs = (
            f32(rows, width),
            f32(1, rows),
            f32(rows, width),
            f32(1, rows),
            f32(2, width // 4, 4, 128),
        )
        args = (idx, left, accum, right, right_accum, relation, grad)
    return pl.pallas_call(
        functools.partial(bucket_kernel, bucket, nbatch),
        out_shape=outs,
        in_specs=[pl.BlockSpec(memory_space=pltpu.VMEM)] * len(args),
        out_specs=[pl.BlockSpec(memory_space=pltpu.VMEM)] * len(outs),
        scratch_shapes=[
            pltpu.VMEM((width, nrel * rows), BF),
            pltpu.VMEM((rows, nrel * rows), F32),
            pltpu.VMEM((rows, nrel * rows), F32),
            pltpu.VMEM((width, nrel * rows), BF),
        ],
        compiler_params=pltpu.CompilerParams(vmem_limit_bytes=40 << 20),
        name=f"bucket{bucket}",
    )(*args)


def final_kernel(total_ref, relation_ref, state_ref, relation_out, state_out):
    nrel, width, _ = relation_ref.shape
    for r in range(nrel):
        for half in range(2):
            cols = slice(half * 128, (half + 1) * 128)
            grad = total_ref[r, half].reshape(width, 128)
            state = state_ref[r, :, cols] + grad * grad
            state_out[r, :, cols] = state
            relation_out[r, :, cols] = relation_ref[r, :, cols] - learn_rate * grad / jnp.sqrt(state)


def final_update(total, relation, state):
    shape = jax.ShapeDtypeStruct(relation.shape, F32)
    return pl.pallas_call(
        final_kernel,
        out_shape=(shape, shape),
        in_specs=[pl.BlockSpec(memory_space=pltpu.VMEM)] * 3,
        out_specs=[pl.BlockSpec(memory_space=pltpu.VMEM)] * 2,
        name="final_update",
    )(total, relation, state)


BLK = ("z", "y", "xl")
REP = ("xh", "core")


def body(
    left_emb,
    left_state,
    right_emb,
    right_state,
    relation,
    relation_state,
    edge_src,
    edge_dst,
    edge_rel,
    negatives,
    batch_counts,
):
    nbatch, batch = edge_src.shape[3:]
    rows, width = left_emb.shape
    blocks = lax.axis_size(BLK)
    index = jnp.stack([edge_src[0, 0], edge_dst[0, 0], edge_rel[0, 0], negatives[0, 0]], axis=2)
    index = index.reshape(8 * nbatch, batch)
    live = jnp.broadcast_to(batch_counts.reshape(2, 1), (2, batch))
    pad = -(8 * nbatch + 2) % 8
    index = jnp.concatenate([index, live, jnp.zeros((pad, batch), jnp.int32)], axis=0)
    index = lax.all_gather(index, REP, axis=0, tiled=False)

    left, right, right_accum, grad = run_bucket(
        0, nbatch, index, left_emb, left_state.reshape(1, rows), right_emb, right_state.reshape(1, rows), relation
    )
    left = lax.ppermute(left, BLK, [(i, (i + 1) % blocks) for i in range(blocks)])
    left, left_accum, right, right_accum, grad = run_bucket(
        1, nbatch, index, left, left, right, right_accum, relation, grad
    )
    grad = grad.reshape(blocks, -1, 128)
    grad = jnp.sum(lax.all_to_all(grad, BLK, 0, 0, tiled=True), axis=0)
    grad = jnp.broadcast_to(grad[None], (blocks, *grad.shape))
    grad = lax.all_to_all(grad, BLK, 0, 0, tiled=True)
    grad = lax.all_gather(grad, "core", axis=0, tiled=False)
    grad = grad.reshape(relation.shape[0], 2, width // 4, 4, 128)
    relation_new, relation_state_new = final_update(grad, relation, relation_state)
    return (
        left,
        left_accum.reshape(rows),
        right,
        right_accum.reshape(rows),
        relation_new,
        relation_state_new,
    )


def solution(mesh):
    sizes = (8, 8, 2, 2, 2)
    mesh = jax.sharding.Mesh(mesh.devices.reshape(sizes), (*BLK, *REP))
    row, edge = P(BLK, None), P(BLK, REP, None, None, None)
    in_specs = (row, P(BLK), row, P(BLK), P(), P(), edge, edge, edge, edge, P(BLK, REP, None))
    out_specs = (row, P(BLK), row, P(BLK), P(), P())
    return jax.shard_map(body, mesh=mesh, in_specs=in_specs, out_specs=out_specs, check_vma=False)
```

```python
import functools

import jax
import jax.numpy as jnp
from jax import lax
from jax.experimental import pallas as pl
from jax.experimental.pallas import tpu as pltpu
from jax.sharding import PartitionSpec as P

learn_rate = 0.1
BF = jnp.bfloat16
F32 = jnp.float32
BLK = ("z", "y", "xl")
REP = ("xh", "core")
SLOTS = 4


def dot(a, b, dims):
    return lax.dot_general(a, b, ((dims[:1], dims[1:]), ((), ())), preferred_element_type=F32)


def same(size):
    shape = (size, size)
    return lax.broadcasted_iota(jnp.int32, shape, 0) == lax.broadcasted_iota(jnp.int32, shape, 1)


def to_column(row):
    return jnp.sum(jnp.where(same(row.shape[1]), row, 0.0), axis=1, keepdims=True)


def to_row(column):
    return jnp.sum(jnp.where(same(column.shape[0]), column, 0.0), axis=0, keepdims=True)


def one_hot(index_row, count):
    rows = lax.broadcasted_iota(jnp.int16, (count, index_row.shape[1]), 0)
    return jnp.where(rows == index_row.astype(jnp.int16), BF(1.0), BF(0.0))


def row_update(embedding, accum, gradient):
    accum = accum + jnp.mean(gradient * gradient, axis=1, keepdims=True)
    return embedding - learn_rate * gradient / jnp.sqrt(accum), accum


def count_batch(idx_ref, member, base, rows, pairs):
    source = idx_ref[member, pl.ds(base, 1), :]
    target = idx_ref[member, pl.ds(base + 1, 1), :]
    relation = idx_ref[member, pl.ds(base + 2, 1), :]
    negative = idx_ref[member, pl.ds(base + 3, 1), :]
    edges = dot(one_hot(target, rows), one_hot(relation * rows + source, pairs), (1, 1))
    counts = dot(one_hot(negative, rows), jnp.ones((negative.shape[1], 128), BF), (1, 0))
    return edges, counts


def each_live_batch(idx_ref, bucket, nbatch, step):
    def member_step(member, slot):
        live = jnp.max(idx_ref[member, pl.ds(8 * nbatch + bucket, 1), :])

        def batch_step(batch, slot):
            step(member, (bucket * nbatch + batch) * 4, slot)
            return slot + 1

        return lax.fori_loop(0, live, batch_step, slot)

    lax.fori_loop(0, idx_ref.shape[0], member_step, 0)


def score_grad(scores_t, edges_of, counts, total):
    for start in range(0, scores_t.shape[1], 128):
        cols = slice(start, start + 128)
        score = scores_t[:, cols]
        top = jnp.max(jnp.where(counts > 0.0, score, -3.0e38), axis=0, keepdims=True)
        above = score - top
        small = jnp.exp(-jnp.abs(above))
        weighted = counts * small
        neg_total = jnp.sum(weighted, axis=0, keepdims=True)
        neg_scale = jnp.where(above > 0.0, small, 1.0)
        pos_exp = jnp.where(above > 0.0, 1.0, small)
        factor = edges_of(cols) * neg_scale / (pos_exp + neg_total * neg_scale)
        factor_sum = jnp.sum(factor, axis=0, keepdims=True)
        total[:, cols] += weighted * factor_sum - neg_total * factor


def queries_and_scores(left_bf, right_bf, op_ref, query_t, scores_t):
    rows = left_bf.shape[0]
    for r in range(op_ref.shape[0]):
        cols = slice(r * rows, (r + 1) * rows)
        query = dot(op_ref[r].astype(BF), left_bf, (1, 1)).astype(BF)
        query_t[:, cols] = query
        scores_t[:, cols] = dot(right_bf, query, (1, 0))


def first_kernel(nbatch, idx_ref, left_ref, accum_ref, right_ref, op_ref, left_out, query_t, grad_bf, scores_t, total):
    nrel = op_ref.shape[0]
    rows, width = left_ref.shape
    half = rows // 2
    right_bf = right_ref[...].astype(BF)
    queries_and_scores(left_ref[...].astype(BF), right_bf, op_ref, query_t, scores_t)
    total[...] = jnp.zeros_like(total)

    def step(member, base, slot):
        edges, counts = count_batch(idx_ref, member, base, rows, nrel * rows)
        score_grad(scores_t, lambda cols: edges[:, cols], counts, total)

    each_live_batch(idx_ref, 0, nbatch, step)
    grad_bf[...] = total[...].astype(BF)
    first = lax.axis_index("core") * half
    left_grad = jnp.zeros((half, width), F32)
    for r in range(nrel):
        cols = pl.ds(pl.multiple_of(r * rows + first, half), half)
        table_t = dot(right_bf, grad_bf[:, cols], (0, 0)).astype(BF)
        left_grad += dot(table_t, op_ref[r].astype(BF), (0, 0))
    mine = pl.ds(pl.multiple_of(first, half), half)
    accum = to_column(accum_ref[:, mine])
    left_out[0:half, :], accum = row_update(left_ref[mine, :], accum, left_grad)
    accum = jnp.concatenate([to_row(accum)] * (width // half), axis=1)
    left_out[half : half + 8, :] = jnp.broadcast_to(accum, (8, width))


def between_kernel(
    nbatch, idx_ref, left_ref, right_ref, accum_ref, query_t, grad_bf, op_ref, right_out, accum_out, grad_out, edges_out, counts_out
):
    rows = right_ref.shape[0]
    pairs = query_t.shape[1]

    def step(member, base, slot):
        edges_out[slot], counts_out[slot] = count_batch(idx_ref, member, base, rows, pairs)

    each_live_batch(idx_ref, 1, nbatch, step)
    right = right_ref[...]
    right_grad = dot(grad_bf[...], query_t[...], (1, 1))
    cols = pl.ds(pl.multiple_of(lax.axis_index("core") * rows, rows), rows)
    table_t = dot(right.astype(BF), grad_bf[:, cols], (0, 0)).astype(BF)
    grad_out[...] = dot(table_t, left_ref[...].astype(BF), (1, 0))
    right_out[...], accum = row_update(right, to_column(accum_ref[...]), right_grad)
    accum_out[...] = to_row(accum)


def second_kernel(
    nbatch, idx_ref, edges_ref, counts_ref, left_ref, right_ref, accum_ref, op_ref, grad_ref,
    left_out, left_accum_out, right_out, right_accum_out, grad_out, query_t, scores_t, total, grad_bf, table_t
):
    nrel = op_ref.shape[0]
    rows, width = right_ref.shape
    half = rows // 2
    left = jnp.concatenate([left_ref[0, 0:half, :], left_ref[1, 0:half, :]], axis=0)
    left_accum = jnp.concatenate([left_ref[0, half : half + 1, 0:half], left_ref[1, half : half + 1, 0:half]], axis=1)
    right = right_ref[...]
    left_bf, right_bf = left.astype(BF), right.astype(BF)
    queries_and_scores(left_bf, right_bf, op_ref, query_t, scores_t)
    total[...] = jnp.zeros_like(total)
    live = 0
    for member in range(idx_ref.shape[0]):
        live += idx_ref[member, 8 * nbatch + 1 : 8 * nbatch + 2, :]

    def step(slot, _):
        score_grad(scores_t, lambda cols: edges_ref[slot, :, cols], counts_ref[slot], total)
        return 0

    lax.fori_loop(0, jnp.max(live), step, 0)
    grad_bf[...] = total[...].astype(BF)
    table_t[...] = dot(right_bf, grad_bf[...], (0, 0)).astype(BF)
    mine = pl.ds(pl.multiple_of(lax.axis_index("core") * rows, rows), rows)
    grad = dot(table_t[:, mine], left_bf, (1, 0)) + grad_ref[...]
    for part in range(2):
        grad_out[part] = grad[:, part * 128 : (part + 1) * 128].reshape(grad_out.shape[1:])
    left_grad = jnp.zeros((rows, width), F32)
    for r in range(nrel):
        left_grad += dot(table_t[:, r * rows : (r + 1) * rows], op_ref[r].astype(BF), (0, 0))
    left_out[...], accum = row_update(left, to_column(left_accum), left_grad)
    left_accum_out[...] = to_row(accum)
    right_grad = dot(grad_bf[...], query_t[...], (1, 1))
    right_out[...], accum = row_update(right, to_column(accum_ref[...]), right_grad)
    right_accum_out[...] = to_row(accum)


def final_kernel(total_ref, relation_ref, state_ref, relation_out, state_out):
    nrel, width, _ = relation_ref.shape
    for r in range(nrel):
        for part in range(2):
            cols = slice(part * 128, (part + 1) * 128)
            grad = total_ref[r, part].reshape(width, 128)
            state = state_ref[r, :, cols] + grad * grad
            state_out[r, :, cols] = state
            relation_out[r, :, cols] = relation_ref[r, :, cols] - learn_rate * grad / jnp.sqrt(state)


def f32(*shape):
    return jax.ShapeDtypeStruct(shape, F32)


def call(kernel, name, outs, args, scratch=(), flops=0):
    return pl.pallas_call(
        kernel,
        out_shape=outs,
        in_specs=[pl.BlockSpec(memory_space=pltpu.VMEM)] * len(args),
        out_specs=[pl.BlockSpec(memory_space=pltpu.VMEM)] * len(outs),
        scratch_shapes=[pltpu.VMEM(shape, dtype) for shape, dtype in scratch],
        compiler_params=pltpu.CompilerParams(vmem_limit_bytes=30 << 20),
        cost_estimate=pl.CostEstimate(flops=flops, bytes_accessed=4 << 20, transcendentals=0),
        name=name,
    )(*args)


def buckets(index, left, left_accum, right, right_accum, relation, nbatch, move):
    nrel, width, _ = relation.shape
    rows = left.shape[0]
    pairs = nrel * rows
    pair_bf = jax.ShapeDtypeStruct((rows, pairs), BF)
    left_half, query_t, grad_bf = call(
        functools.partial(first_kernel, nbatch),
        "bucket0_left",
        (f32(rows // 2 + 8, width), jax.ShapeDtypeStruct((width, pairs), BF), pair_bf),
        (index, left, left_accum, right, relation),
        [((rows, pairs), F32), ((rows, pairs), F32)],
        flops=2 << 30,
    )
    moved = move(left_half)
    right, right_accum, grad, edges, counts = call(
        functools.partial(between_kernel, nbatch),
        "bucket0_right",
        (f32(rows, width), f32(1, rows), f32(width, width), f32(SLOTS, rows, pairs), f32(SLOTS, rows, 128)),
        (index, left, right, right_accum, query_t, grad_bf, relation),
        flops=1 << 30,
    )
    moved = lax.all_gather(moved, "core", axis=0, tiled=False)
    return call(
        functools.partial(second_kernel, nbatch),
        "bucket1",
        (f32(rows, width), f32(1, rows), f32(rows, width), f32(1, rows), f32(2, width // 4, 4, 128)),
        (index, edges, counts, moved, right, right_accum, relation, grad),
        [((width, pairs), BF), ((rows, pairs), F32), ((rows, pairs), F32), ((rows, pairs), BF), ((width, pairs), BF)],
        flops=2 << 30,
    )


def body(
    left_emb,
    left_state,
    right_emb,
    right_state,
    relation,
    relation_state,
    edge_src,
    edge_dst,
    edge_rel,
    negatives,
    batch_counts,
):
    nbatch, batch = edge_src.shape[3:]
    rows, width = left_emb.shape
    blocks = lax.axis_size(BLK)
    index = jnp.stack([edge_src[0, 0], edge_dst[0, 0], edge_rel[0, 0], negatives[0, 0]], axis=2)
    index = index.reshape(8 * nbatch, batch)
    live = jnp.broadcast_to(batch_counts.reshape(2, 1), (2, batch))
    pad = -(8 * nbatch + 2) % 8
    index = jnp.concatenate([index, live, jnp.zeros((pad, batch), jnp.int32)], axis=0)
    index = lax.all_gather(index, REP, axis=0, tiled=False)
    route = [(i, (i + 1) % blocks) for i in range(blocks)]
    left, left_accum, right, right_accum, grad = buckets(
        index,
        left_emb,
        left_state.reshape(1, rows),
        right_emb,
        right_state.reshape(1, rows),
        relation,
        nbatch,
        lambda half: lax.ppermute(half, BLK, route),
    )
    grad = grad.reshape(blocks, -1, 128)
    grad = jnp.sum(lax.all_to_all(grad, BLK, 0, 0, tiled=True), axis=0)
    grad = jnp.broadcast_to(grad[None], (blocks, *grad.shape))
    grad = lax.all_to_all(grad, BLK, 0, 0, tiled=True)
    grad = lax.all_gather(grad, "core", axis=0, tiled=False)
    grad = grad.reshape(relation.shape[0], 2, width // 4, 4, 128)
    relation_new, relation_state_new = call(
        final_kernel, "final_update", (f32(*relation.shape),) * 2, (grad, relation, relation_state)
    )
    return (
        left,
        left_accum.reshape(rows),
        right,
        right_accum.reshape(rows),
        relation_new,
        relation_state_new,
    )


def solution(mesh):
    sizes = (8, 8, 2, 2, 2)
    mesh = jax.sharding.Mesh(mesh.devices.reshape(sizes), (*BLK, *REP))
    row, edge = P(BLK, None), P(BLK, REP, None, None, None)
    in_specs = (row, P(BLK), row, P(BLK), P(), P(), edge, edge, edge, edge, P(BLK, REP, None))
    out_specs = (row, P(BLK), row, P(BLK), P(), P())
    return jax.shard_map(body, mesh=mesh, in_specs=in_specs, out_specs=out_specs, check_vma=False)
```

```python
import functools

import jax
import jax.numpy as jnp
from jax import lax
from jax.experimental import pallas as pl
from jax.experimental.pallas import tpu as pltpu
from jax.sharding import PartitionSpec as P

learn_rate = 0.1
BF = jnp.bfloat16
F32 = jnp.float32
BLK = ("z", "y", "xl")
REP = ("xh", "core")
SLOTS = 4


def dot(a, b, dims):
    return lax.dot_general(a, b, ((dims[:1], dims[1:]), ((), ())), preferred_element_type=F32)


def same(size):
    shape = (size, size)
    return lax.broadcasted_iota(jnp.int32, shape, 0) == lax.broadcasted_iota(jnp.int32, shape, 1)


def to_column(row):
    return jnp.sum(jnp.where(same(row.shape[1]), row, 0.0), axis=1, keepdims=True)


def to_row(column):
    return jnp.sum(jnp.where(same(column.shape[0]), column, 0.0), axis=0, keepdims=True)


def one_hot(index_row, count):
    rows = lax.broadcasted_iota(jnp.int16, (count, index_row.shape[1]), 0)
    return jnp.where(rows == index_row.astype(jnp.int16), BF(1.0), BF(0.0))


def row_update(embedding, accum, gradient):
    accum = accum + jnp.mean(gradient * gradient, axis=1, keepdims=True)
    return embedding - learn_rate * gradient / jnp.sqrt(accum), accum


def count_batch(idx_ref, member, base, rows, pairs):
    source = idx_ref[member, pl.ds(base, 1), :]
    target = idx_ref[member, pl.ds(base + 1, 1), :]
    relation = idx_ref[member, pl.ds(base + 2, 1), :]
    negative = idx_ref[member, pl.ds(base + 3, 1), :]
    edges = dot(one_hot(target, rows), one_hot(relation * rows + source, pairs), (1, 1))
    counts = dot(one_hot(negative, rows), jnp.ones((negative.shape[1], 128), BF), (1, 0))
    return edges, counts


def each_live_batch(idx_ref, bucket, nbatch, step):
    def member_step(member, slot):
        live = jnp.max(idx_ref[member, pl.ds(8 * nbatch + bucket, 1), :])

        def batch_step(batch, slot):
            step(member, (bucket * nbatch + batch) * 4, slot)
            return slot + 1

        return lax.fori_loop(0, live, batch_step, slot)

    return lax.fori_loop(0, idx_ref.shape[0], member_step, 0)


def score_grad(scores_t, edges_of, counts, total):
    for start in range(0, scores_t.shape[1], 128):
        cols = slice(start, start + 128)
        score = scores_t[:, cols]
        top = jnp.max(jnp.where(counts > 0.0, score, -3.0e38), axis=0, keepdims=True)
        above = score - top
        small = jnp.exp(-jnp.abs(above))
        weighted = counts * small
        neg_total = jnp.sum(weighted, axis=0, keepdims=True)
        neg_scale = jnp.where(above > 0.0, small, 1.0)
        pos_exp = jnp.where(above > 0.0, 1.0, small)
        factor = edges_of(cols) * neg_scale / (pos_exp + neg_total * neg_scale)
        factor_sum = jnp.sum(factor, axis=0, keepdims=True)
        total[:, cols] += weighted * factor_sum - neg_total * factor


def queries_and_scores(left_bf, right_bf, op_ref, query_t, scores_t):
    rows = left_bf.shape[0]
    for r in range(op_ref.shape[0]):
        cols = slice(r * rows, (r + 1) * rows)
        query = dot(op_ref[r].astype(BF), left_bf, (1, 1)).astype(BF)
        query_t[:, cols] = query
        scores_t[:, cols] = dot(right_bf, query, (1, 0))


def gather_kernel(nbatch, *refs):
    sources, out_ref, buffers, sems = refs[:5], refs[5], refs[6:11], refs[11]
    copies = [pltpu.make_async_copy(a, b, sems.at[i]) for i, (a, b) in enumerate(zip(sources, buffers))]
    for copy in copies:
        copy.start()
    out_ref[8 * nbatch :, :] = jnp.zeros_like(out_ref[8 * nbatch :, :])
    for copy in copies:
        copy.wait()
    *buffers, live_ref = buffers
    for bucket in range(2):
        row = 8 * nbatch + bucket
        out_ref[row : row + 1, :] = jnp.full((1, out_ref.shape[1]), live_ref[0, 0, bucket])
    for bucket in range(2):
        for batch in range(nbatch):
            for i, buffer in enumerate(buffers):
                row = (bucket * nbatch + batch) * 4 + i
                out_ref[row : row + 1, :] = buffer[0, 0, bucket, batch : batch + 1, :]


def first_kernel(nbatch, idx_ref, left_hbm, accum_hbm, right_hbm, op_hbm, left_out, query_t, grad_bf, left_ref, accum_ref, right_ref, op_ref, scores_t, total, edges_ref, counts_ref, sems):
    pairs = ((op_hbm, op_ref), (left_hbm, left_ref), (right_hbm, right_ref), (accum_hbm, accum_ref))
    copies = [pltpu.make_async_copy(*pair, sems.at[i]) for i, pair in enumerate(pairs)]
    for copy in copies:
        copy.start()
    nrel = op_ref.shape[0]
    rows, width = left_ref.shape
    half = rows // 2

    def count(member, base, slot):
        edges_ref[slot], counts_ref[slot] = count_batch(idx_ref, member, base, rows, nrel * rows)

    live = each_live_batch(idx_ref, 0, nbatch, count)
    for copy in copies:
        copy.wait()
    right_bf = right_ref[...].astype(BF)
    queries_and_scores(left_ref[...].astype(BF), right_bf, op_ref, query_t, scores_t)
    total[...] = jnp.zeros_like(total)

    def step(slot, _):
        score_grad(scores_t, lambda cols: edges_ref[slot, :, cols], counts_ref[slot], total)
        return 0

    lax.fori_loop(0, live, step, 0)
    grad_bf[...] = total[...].astype(BF)
    first = lax.axis_index("core") * half
    left_grad = jnp.zeros((half, width), F32)
    for r in range(nrel):
        cols = pl.ds(pl.multiple_of(r * rows + first, half), half)
        table_t = dot(right_bf, grad_bf[:, cols], (0, 0)).astype(BF)
        left_grad += dot(table_t, op_ref[r].astype(BF), (0, 0))
    mine = pl.ds(pl.multiple_of(first, half), half)
    accum = to_column(accum_ref[:, mine])
    left_out[0:half, :], accum = row_update(left_ref[mine, :], accum, left_grad)
    accum = jnp.concatenate([to_row(accum)] * (width // half), axis=1)
    left_out[half : half + 8, :] = jnp.broadcast_to(accum, (8, width))


def between_kernel(
    nbatch, idx_ref, left_ref, right_ref, accum_ref, query_t, grad_bf, op_ref, right_out, accum_out, grad_out, edges_out, counts_out
):
    rows = right_ref.shape[0]
    pairs = query_t.shape[1]

    def step(member, base, slot):
        edges_out[slot], counts_out[slot] = count_batch(idx_ref, member, base, rows, pairs)

    each_live_batch(idx_ref, 1, nbatch, step)
    right = right_ref[...]
    right_grad = dot(grad_bf[...], query_t[...], (1, 1))
    cols = pl.ds(pl.multiple_of(lax.axis_index("core") * rows, rows), rows)
    table_t = dot(right.astype(BF), grad_bf[:, cols], (0, 0)).astype(BF)
    grad_out[...] = dot(table_t, left_ref[...].astype(BF), (1, 0))
    right_out[...], accum = row_update(right, to_column(accum_ref[...]), right_grad)
    accum_out[...] = to_row(accum)


def second_kernel(
    nbatch, idx_ref, edges_ref, counts_ref, left_ref, right_ref, accum_ref, op_ref, grad_ref,
    left_out, left_accum_out, right_out, right_accum_out, grad_out, query_t, scores_t, total, grad_bf, table_t
):
    nrel = op_ref.shape[0]
    rows, width = right_ref.shape
    half = rows // 2
    left = jnp.concatenate([left_ref[0, 0:half, :], left_ref[1, 0:half, :]], axis=0)
    left_accum = jnp.concatenate([left_ref[0, half : half + 1, 0:half], left_ref[1, half : half + 1, 0:half]], axis=1)
    right = right_ref[...]
    left_bf, right_bf = left.astype(BF), right.astype(BF)
    queries_and_scores(left_bf, right_bf, op_ref, query_t, scores_t)
    total[...] = jnp.zeros_like(total)
    live = 0
    for member in range(idx_ref.shape[0]):
        live += idx_ref[member, 8 * nbatch + 1 : 8 * nbatch + 2, :]

    def step(slot, _):
        score_grad(scores_t, lambda cols: edges_ref[slot, :, cols], counts_ref[slot], total)
        return 0

    lax.fori_loop(0, jnp.max(live), step, 0)
    grad_bf[...] = total[...].astype(BF)
    table_t[...] = dot(right_bf, grad_bf[...], (0, 0)).astype(BF)
    mine = pl.ds(pl.multiple_of(lax.axis_index("core") * rows, rows), rows)
    grad = dot(table_t[:, mine], left_bf, (1, 0)) + grad_ref[...]
    for part in range(2):
        grad_out[part] = grad[:, part * 128 : (part + 1) * 128].reshape(grad_out.shape[1:])
    left_grad = jnp.zeros((rows, width), F32)
    for r in range(nrel):
        left_grad += dot(table_t[:, r * rows : (r + 1) * rows], op_ref[r].astype(BF), (0, 0))
    left_out[...], accum = row_update(left, to_column(left_accum), left_grad)
    left_accum_out[...] = to_row(accum)
    right_grad = dot(grad_bf[...], query_t[...], (1, 1))
    right_out[...], accum = row_update(right, to_column(accum_ref[...]), right_grad)
    right_accum_out[...] = to_row(accum)


def final_kernel(total_ref, relation_ref, state_ref, relation_out, state_out):
    nrel, width, _ = relation_ref.shape
    for r in range(nrel):
        for part in range(2):
            cols = slice(part * 128, (part + 1) * 128)
            grad = total_ref[r, part].reshape(width, 128)
            state = state_ref[r, :, cols] + grad * grad
            state_out[r, :, cols] = state
            relation_out[r, :, cols] = relation_ref[r, :, cols] - learn_rate * grad / jnp.sqrt(state)


def f32(*shape):
    return jax.ShapeDtypeStruct(shape, F32)


def call(kernel, name, outs, args, scratch=(), flops=0, outside=()):
    spaces = [pltpu.HBM if i in outside else pltpu.VMEM for i in range(len(args))]
    sems = [pltpu.SemaphoreType.DMA((len(outside),))] if outside else []
    return pl.pallas_call(
        kernel,
        out_shape=outs,
        in_specs=[pl.BlockSpec(memory_space=space) for space in spaces],
        out_specs=[pl.BlockSpec(memory_space=pltpu.VMEM)] * len(outs),
        scratch_shapes=[pltpu.VMEM(*one) if isinstance(one, tuple) else one for one in scratch] + sems,
        compiler_params=pltpu.CompilerParams(vmem_limit_bytes=30 << 20),
        cost_estimate=pl.CostEstimate(flops=flops, bytes_accessed=4 << 20, transcendentals=0),
        name=name,
    )(*(pltpu.with_memory_space_constraint(a, pltpu.HBM) if i in outside else a for i, a in enumerate(args)))


def buckets(index, left, left_accum, right, right_accum, relation, nbatch, move):
    nrel, width, _ = relation.shape
    rows = left.shape[0]
    pairs = nrel * rows
    pair_bf = jax.ShapeDtypeStruct((rows, pairs), BF)
    left_half, query_t, grad_bf = call(
        functools.partial(first_kernel, nbatch),
        "bucket0_left",
        (f32(rows // 2 + 8, width), jax.ShapeDtypeStruct((width, pairs), BF), pair_bf),
        (index, left, left_accum, right, relation),
        [((rows, width), F32), ((1, rows), F32), ((rows, width), F32), (relation.shape, F32), ((rows, pairs), F32), ((rows, pairs), F32),
         ((SLOTS, rows, pairs), F32), ((SLOTS, rows, 128), F32)],
        flops=2 << 30,
        outside=(1, 2, 3, 4),
    )
    moved = move(left_half)
    right, right_accum, grad, edges, counts = call(
        functools.partial(between_kernel, nbatch),
        "bucket0_right",
        (f32(rows, width), f32(1, rows), f32(width, width), f32(SLOTS, rows, pairs), f32(SLOTS, rows, 128)),
        (index, left, right, right_accum, query_t, grad_bf, relation),
        flops=1 << 30,
    )
    moved = lax.all_gather(moved, "core", axis=0, tiled=False)
    return call(
        functools.partial(second_kernel, nbatch),
        "bucket1",
        (f32(rows, width), f32(1, rows), f32(rows, width), f32(1, rows), f32(2, width // 4, 4, 128)),
        (index, edges, counts, moved, right, right_accum, relation, grad),
        [((width, pairs), BF), ((rows, pairs), F32), ((rows, pairs), F32), ((rows, pairs), BF), ((width, pairs), BF)],
        flops=2 << 30,
    )


def body(
    left_emb,
    left_state,
    right_emb,
    right_state,
    relation,
    relation_state,
    edge_src,
    edge_dst,
    edge_rel,
    negatives,
    batch_counts,
):
    nbatch, batch = edge_src.shape[3:]
    rows, width = left_emb.shape
    blocks = lax.axis_size(BLK)
    index_rows = -(-(8 * nbatch + 2) // 8) * 8
    index = call(
        functools.partial(gather_kernel, nbatch),
        "gather_index",
        (jax.ShapeDtypeStruct((index_rows, batch), jnp.int32),),
        (edge_src, edge_dst, edge_rel, negatives, batch_counts),
        [(edge_src.shape, jnp.int32)] * 4 + [pltpu.SMEM(batch_counts.shape, jnp.int32)],
        outside=(0, 1, 2, 3, 4),
    )[0]
    index = lax.all_gather(index, REP, axis=0, tiled=False)
    route = [(i, (i + 1) % blocks) for i in range(blocks)]
    left, left_accum, right, right_accum, grad = buckets(
        index,
        left_emb,
        left_state.reshape(1, rows),
        right_emb,
        right_state.reshape(1, rows),
        relation,
        nbatch,
        lambda half: lax.ppermute(half, BLK, route),
    )
    grad = grad.reshape(blocks, -1, 128)
    grad = jnp.sum(lax.all_to_all(grad, BLK, 0, 0, tiled=True), axis=0)
    grad = jnp.broadcast_to(grad[None], (blocks, *grad.shape))
    grad = lax.all_to_all(grad, BLK, 0, 0, tiled=True)
    grad = lax.all_gather(grad, "core", axis=0, tiled=False)
    grad = grad.reshape(relation.shape[0], 2, width // 4, 4, 128)
    relation_new, relation_state_new = call(
        final_kernel, "final_update", (f32(*relation.shape),) * 2, (grad, relation, relation_state)
    )
    return (
        left,
        left_accum.reshape(rows),
        right,
        right_accum.reshape(rows),
        relation_new,
        relation_state_new,
    )


def solution(mesh):
    sizes = (8, 8, 2, 2, 2)
    mesh = jax.sharding.Mesh(mesh.devices.reshape(sizes), (*BLK, *REP))
    row, edge = P(BLK, None), P(BLK, REP, None, None, None)
    in_specs = (row, P(BLK), row, P(BLK), P(), P(), edge, edge, edge, edge, P(BLK, REP, None))
    out_specs = (row, P(BLK), row, P(BLK), P(), P())
    return jax.shard_map(body, mesh=mesh, in_specs=in_specs, out_specs=out_specs, check_vma=False)
```

```python
import functools

import jax
import jax.numpy as jnp
from jax import lax
from jax.experimental import pallas as pl
from jax.experimental.pallas import tpu as pltpu
from jax.sharding import PartitionSpec as P

learn_rate = 0.1
BF = jnp.bfloat16
F32 = jnp.float32
BLK = ("z", "y", "xl")
REP = ("xh", "core")
NREL = 2
SLOTS = 4


def dot(a, b, dims):
    return lax.dot_general(a, b, ((dims[:1], dims[1:]), ((), ())), preferred_element_type=F32)


def same(size):
    shape = (size, size)
    return lax.broadcasted_iota(jnp.int32, shape, 0) == lax.broadcasted_iota(jnp.int32, shape, 1)


def to_column(row):
    return jnp.sum(jnp.where(same(row.shape[1]), row, 0.0), axis=1, keepdims=True)


def to_row(column):
    return jnp.sum(jnp.where(same(column.shape[0]), column, 0.0), axis=0, keepdims=True)


def one_hot(index_row, count):
    rows = lax.broadcasted_iota(jnp.int16, (count, index_row.shape[1]), 0)
    return jnp.where(rows == index_row.astype(jnp.int16), BF(1.0), BF(0.0))


def row_update(embedding, accum, gradient):
    accum = accum + jnp.mean(gradient * gradient, axis=1, keepdims=True)
    return embedding - learn_rate * gradient / jnp.sqrt(accum), accum


def count_batch(idx_ref, member, base, rows, half, first):
    source = idx_ref[member, pl.ds(base, 1), :] - first
    target = idx_ref[member, pl.ds(base + 1, 1), :]
    relation = idx_ref[member, pl.ds(base + 2, 1), :]
    negative = idx_ref[member, pl.ds(base + 3, 1), :]
    pair = jnp.where((source >= 0) & (source < half), relation * half + source, -1)
    edges = dot(one_hot(target, rows), one_hot(pair, NREL * half), (1, 1))
    counts = dot(one_hot(negative, rows), jnp.ones((negative.shape[1], 128), BF), (1, 0))
    return edges, counts


def each_live_batch(idx_ref, bucket, nbatch, step):
    members = idx_ref.shape[0]
    row = 8 * nbatch + bucket
    ends = [jnp.max(idx_ref[member, row : row + 1, :]) for member in range(members)]
    for member in range(1, members):
        ends[member] = ends[member] + ends[member - 1]

    def slot_step(slot, _):
        member, begin = jnp.int32(0), jnp.int32(0)
        for end in ends[:-1]:
            member = member + jnp.where(slot >= end, 1, 0)
            begin = jnp.where(slot >= end, end, begin)
        step(member, (bucket * nbatch + slot - begin) * 4, slot)
        return 0

    lax.fori_loop(0, ends[-1], slot_step, 0)
    return ends[-1]


def score_grad(scores_t, edges_of, counts, total):
    for start in range(0, scores_t.shape[1], 128):
        cols = slice(start, start + 128)
        score = scores_t[:, cols]
        top = jnp.max(jnp.where(counts > 0.0, score, -3.0e38), axis=0, keepdims=True)
        above = score - top
        small = jnp.exp(-jnp.abs(above))
        weighted = counts * small
        neg_total = jnp.sum(weighted, axis=0, keepdims=True)
        neg_scale = jnp.where(above > 0.0, small, 1.0)
        pos_exp = jnp.where(above > 0.0, 1.0, small)
        factor = edges_of(cols) * neg_scale / (pos_exp + neg_total * neg_scale)
        factor_sum = jnp.sum(factor, axis=0, keepdims=True)
        total[:, cols] += weighted * factor_sum - neg_total * factor


def queries_and_scores(left_bf, right_bf, op_ref, query_t, scores_t):
    half = left_bf.shape[0]
    for r in range(NREL):
        cols = slice(r * half, (r + 1) * half)
        query_t[:, cols] = dot(op_ref[r].astype(BF), left_bf, (1, 1)).astype(BF)
    scores_t[...] = dot(right_bf, query_t[...], (1, 0))


def table_products(table_t, op_ref):
    half = table_t.shape[1] // NREL
    return sum(dot(table_t[:, r * half : (r + 1) * half], op_ref[r].astype(BF), (0, 0)) for r in range(NREL))


def operator_products(table_t, left_bf, r):
    half = left_bf.shape[0]
    return dot(table_t[:, r * half : (r + 1) * half], left_bf, (1, 0))


def pack_rows(out_ref, embedding, accum):
    half, width = embedding.shape
    out_ref[0:half, :] = embedding
    row = jnp.concatenate([to_row(accum)] * (width // half), axis=1)
    out_ref[half : half + 8, :] = jnp.broadcast_to(row, (8, width))


def gather_kernel(nbatch, *refs):
    sources, out_ref, buffers, sems = refs[:5], refs[5], refs[6:11], refs[11]
    copies = [pltpu.make_async_copy(a, b, sems.at[i]) for i, (a, b) in enumerate(zip(sources, buffers))]
    for copy in copies:
        copy.start()
    out_ref[8 * nbatch :, :] = jnp.zeros_like(out_ref[8 * nbatch :, :])
    for copy in copies:
        copy.wait()
    *buffers, live_ref = buffers
    for bucket in range(2):
        row = 8 * nbatch + bucket
        out_ref[row : row + 1, :] = jnp.full((1, out_ref.shape[1]), live_ref[0, 0, bucket])
    for bucket in range(2):
        for batch in range(nbatch):
            for i, buffer in enumerate(buffers):
                row = (bucket * nbatch + batch) * 4 + i
                out_ref[row : row + 1, :] = buffer[0, 0, bucket, batch : batch + 1, :]


def first_kernel(
    nbatch, idx_ref, left_hbm, accum_hbm, right_hbm, op_hbm, left_out, query_t, grad_bf, table_t,
    left_ref, accum_ref, right_ref, op_ref, scores_t, total, edges_ref, counts_ref, sems
):
    rows, width = right_ref.shape
    half = left_ref.shape[0]
    first = pl.multiple_of(lax.axis_index("core") * half, half)
    pairs = (
        (op_hbm, op_ref),
        (left_hbm.at[pl.ds(first, half), :], left_ref),
        (right_hbm, right_ref),
        (accum_hbm, accum_ref),
    )
    copies = [pltpu.make_async_copy(*pair, sems.at[i]) for i, pair in enumerate(pairs)]
    for copy in copies:
        copy.start()

    def count(member, base, slot):
        edges_ref[slot], counts_ref[slot] = count_batch(idx_ref, member, base, rows, half, first)

    live = each_live_batch(idx_ref, 0, nbatch, count)
    for copy in copies:
        copy.wait()
    right_bf = right_ref[...].astype(BF)
    queries_and_scores(left_ref[...].astype(BF), right_bf, op_ref, query_t, scores_t)
    total[...] = jnp.zeros_like(total)

    def step(slot, _):
        score_grad(scores_t, lambda cols: edges_ref[slot, :, cols], counts_ref[slot], total)
        return 0

    lax.fori_loop(0, live, step, 0)
    grad_bf[...] = total[...].astype(BF)
    table_t[...] = dot(right_bf, grad_bf[...], (0, 0)).astype(BF)
    left_grad = table_products(table_t, op_ref)
    accum = to_column(accum_ref[:, pl.ds(first, half)])
    pack_rows(left_out, *row_update(left_ref[...], accum, left_grad))


def between_kernel(nbatch, idx_ref, left_ref, query_t, grad_bf, table_t, right_grad_out, grad_out, edges_out, counts_out):
    rows = query_t.shape[0]
    half = query_t.shape[1] // NREL
    first = pl.multiple_of(lax.axis_index("core") * half, half)
    right_grad_out[...] = dot(grad_bf[...], query_t[...], (1, 1))
    left_bf = left_ref[pl.ds(first, half), :].astype(BF)
    for r in range(NREL):
        grad_out[r] = operator_products(table_t, left_bf, r)

    def count(member, base, slot):
        edges_out[slot], counts_out[slot] = count_batch(idx_ref, member, base, rows, half, first)

    each_live_batch(idx_ref, 1, nbatch, count)


def right_kernel(grads_ref, right_ref, accum_ref, right_out, accum_out):
    grad = grads_ref[0] + grads_ref[1]
    right_out[...], accum = row_update(right_ref[...], to_column(accum_ref[...]), grad)
    accum_out[...] = to_row(accum)


def second_kernel(
    nbatch, idx_ref, edges_ref, counts_ref, left_ref, right_ref, op_ref, grad_ref,
    grad_out, query_t, grad_bf, table_t, scores_t, total
):
    half = query_t.shape[1] // NREL
    left_bf = left_ref[0:half, :].astype(BF)
    right_bf = right_ref[...].astype(BF)
    queries_and_scores(left_bf, right_bf, op_ref, query_t, scores_t)
    total[...] = jnp.zeros_like(total)
    live = 0
    for member in range(idx_ref.shape[0]):
        live += idx_ref[member, 8 * nbatch + 1 : 8 * nbatch + 2, :]

    def step(slot, _):
        score_grad(scores_t, lambda cols: edges_ref[slot, :, cols], counts_ref[slot], total)
        return 0

    lax.fori_loop(0, jnp.max(live), step, 0)
    grad_bf[...] = total[...].astype(BF)
    table_t[...] = dot(right_bf, grad_bf[...], (0, 0)).astype(BF)
    for r in range(NREL):
        grad = operator_products(table_t, left_bf, r) + grad_ref[r]
        for part in range(2):
            grad_out[r, part] = grad[:, part * 128 : (part + 1) * 128].reshape(grad_out.shape[2:])


def last_rows_kernel(left_ref, op_ref, query_t, grad_bf, table_t, out_ref):
    half = left_ref.shape[0] - 8
    accum = to_column(left_ref[half : half + 1, 0:half])
    pack_rows(out_ref, *row_update(left_ref[0:half, :], accum, table_products(table_t, op_ref)))
    out_ref[half + 8 :, :] = dot(grad_bf[...], query_t[...], (1, 1))


def rows_kernel(parts_ref, right_ref, accum_ref, left_out, left_accum_out, right_out, right_accum_out):
    half = left_out.shape[0] // 2
    for part in range(2):
        mine = slice(part * half, (part + 1) * half)
        left_out[mine, :] = parts_ref[part, 0:half, :]
        left_accum_out[:, mine] = parts_ref[part, half : half + 1, 0:half]
    grad = parts_ref[0, half + 8 :, :] + parts_ref[1, half + 8 :, :]
    right_out[...], accum = row_update(right_ref[...], to_column(accum_ref[...]), grad)
    right_accum_out[...] = to_row(accum)


def final_kernel(total_ref, relation_ref, state_ref, relation_out, state_out):
    nrel, width, _ = relation_ref.shape
    for r in range(nrel):
        for part in range(2):
            cols = slice(part * 128, (part + 1) * 128)
            grad = total_ref[r, part].reshape(width, 128)
            state = state_ref[r, :, cols] + grad * grad
            state_out[r, :, cols] = state
            relation_out[r, :, cols] = relation_ref[r, :, cols] - learn_rate * grad / jnp.sqrt(state)


def f32(*shape):
    return jax.ShapeDtypeStruct(shape, F32)


def call(kernel, name, outs, args, scratch=(), flops=0, outside=()):
    spaces = [pltpu.HBM if i in outside else pltpu.VMEM for i in range(len(args))]
    sems = [pltpu.SemaphoreType.DMA((len(outside),))] if outside else []
    return pl.pallas_call(
        kernel,
        out_shape=outs,
        in_specs=[pl.BlockSpec(memory_space=space) for space in spaces],
        out_specs=[pl.BlockSpec(memory_space=pltpu.VMEM)] * len(outs),
        scratch_shapes=[pltpu.VMEM(*one) if isinstance(one, tuple) else one for one in scratch] + sems,
        compiler_params=pltpu.CompilerParams(vmem_limit_bytes=30 << 20),
        cost_estimate=pl.CostEstimate(flops=flops, bytes_accessed=4 << 20, transcendentals=0),
        name=name,
    )(*(pltpu.with_memory_space_constraint(a, pltpu.HBM) if i in outside else a for i, a in enumerate(args)))


def buckets(index, left, left_accum, right, right_accum, relation, nbatch, move):
    width = relation.shape[-1]
    rows = left.shape[0]
    half = rows // 2
    pairs = NREL * half
    bf16 = lambda *shape: jax.ShapeDtypeStruct(shape, BF)
    moved, query_t, grad_bf, table_t = call(
        functools.partial(first_kernel, nbatch),
        "bucket0_left",
        (f32(half + 8, width), bf16(width, pairs), bf16(rows, pairs), bf16(width, pairs)),
        (index, left, left_accum, right, relation),
        [((half, width), F32), ((1, rows), F32), ((rows, width), F32), (relation.shape, F32), ((rows, pairs), F32),
         ((rows, pairs), F32), ((SLOTS, rows, pairs), F32), ((SLOTS, rows, 128), F32)],
        flops=2 << 30,
        outside=(1, 2, 3, 4),
    )
    moved = move(moved)
    right_grad, grad, edges, counts = call(
        functools.partial(between_kernel, nbatch),
        "bucket0_rest",
        (f32(rows, width), f32(NREL, width, width), f32(SLOTS, rows, pairs), f32(SLOTS, rows, 128)),
        (index, left, query_t, grad_bf, table_t),
        flops=1 << 30,
    )
    right_grad = lax.all_gather(right_grad, "core", axis=0, tiled=False)
    right, right_accum = call(
        right_kernel, "bucket0_right", (f32(rows, width), f32(1, rows)), (right_grad, right, right_accum), flops=1 << 28
    )
    grad, query_t, grad_bf, table_t = call(
        functools.partial(second_kernel, nbatch),
        "bucket1",
        (f32(NREL, 2, width // 8, 8, 128), bf16(width, pairs), bf16(rows, pairs), bf16(width, pairs)),
        (index, edges, counts, moved, right, relation, grad),
        [((rows, pairs), F32), ((rows, pairs), F32)],
        flops=2 << 30,
    )
    parts = call(
        last_rows_kernel,
        "bucket1_rows",
        (f32(half + 8 + rows, width),),
        (moved, relation, query_t, grad_bf, table_t),
        flops=1 << 30,
    )[0]
    parts = lax.all_gather(parts, "core", axis=0, tiled=False)
    updated = call(
        rows_kernel,
        "bucket1_right",
        (f32(rows, width), f32(1, rows), f32(rows, width), f32(1, rows)),
        (parts, right, right_accum),
        flops=1 << 28,
    )
    return (*updated, grad)


def body(
    left_emb,
    left_state,
    right_emb,
    right_state,
    relation,
    relation_state,
    edge_src,
    edge_dst,
    edge_rel,
    negatives,
    batch_counts,
):
    nbatch, batch = edge_src.shape[3:]
    rows, width = left_emb.shape
    blocks = lax.axis_size(BLK)
    index_rows = -(-(8 * nbatch + 2) // 8) * 8
    index = call(
        functools.partial(gather_kernel, nbatch),
        "gather_index",
        (jax.ShapeDtypeStruct((index_rows, batch), jnp.int32),),
        (edge_src, edge_dst, edge_rel, negatives, batch_counts),
        [(edge_src.shape, jnp.int32)] * 4 + [pltpu.SMEM(batch_counts.shape, jnp.int32)],
        outside=(0, 1, 2, 3, 4),
    )[0]
    index = lax.all_gather(index, REP, axis=0, tiled=False)
    route = [(i, (i + 1) % blocks) for i in range(blocks)]
    left, left_accum, right, right_accum, grad = buckets(
        index,
        left_emb,
        left_state.reshape(1, rows),
        right_emb,
        right_state.reshape(1, rows),
        relation,
        nbatch,
        lambda half: lax.ppermute(half, BLK, route),
    )
    grad = grad.reshape(blocks, -1, 128)
    grad = jnp.sum(lax.all_to_all(grad, BLK, 0, 0, tiled=True), axis=0)
    grad = jnp.sum(lax.all_gather(grad, "core", axis=0, tiled=False), axis=0)
    grad = jnp.broadcast_to(grad[None], (blocks, *grad.shape))
    grad = lax.all_to_all(grad, BLK, 0, 0, tiled=True)
    grad = grad.reshape(NREL, 2, width // 8, 8, 128)
    relation_new, relation_state_new = call(
        final_kernel, "final_update", (f32(*relation.shape),) * 2, (grad, relation, relation_state)
    )
    return (
        left,
        left_accum.reshape(rows),
        right,
        right_accum.reshape(rows),
        relation_new,
        relation_state_new,
    )


def solution(mesh):
    sizes = (8, 8, 2, 2, 2)
    mesh = jax.sharding.Mesh(mesh.devices.reshape(sizes), (*BLK, *REP))
    row, edge = P(BLK, None), P(BLK, REP, None, None, None)
    in_specs = (row, P(BLK), row, P(BLK), P(), P(), edge, edge, edge, edge, P(BLK, REP, None))
    out_specs = (row, P(BLK), row, P(BLK), P(), P())
    return jax.shard_map(body, mesh=mesh, in_specs=in_specs, out_specs=out_specs, check_vma=False)
```

```python
import functools

import jax
import jax.numpy as jnp
from jax import lax
from jax.experimental import pallas as pl
from jax.experimental.pallas import tpu as pltpu
from jax.sharding import PartitionSpec as P

learn_rate = 0.1
BF = jnp.bfloat16
F32 = jnp.float32
BLK = ("z", "y", "xl")
REP = ("xh", "core")
NREL = 2
SLOTS = 4


def dot(a, b, dims):
    return lax.dot_general(a, b, ((dims[:1], dims[1:]), ((), ())), preferred_element_type=F32)


def same(size):
    shape = (size, size)
    return lax.broadcasted_iota(jnp.int32, shape, 0) == lax.broadcasted_iota(jnp.int32, shape, 1)


def to_column(row):
    return jnp.sum(jnp.where(same(row.shape[1]), row, 0.0), axis=1, keepdims=True)


def to_row(column):
    return jnp.sum(jnp.where(same(column.shape[0]), column, 0.0), axis=0, keepdims=True)


def one_hot(index_row, count):
    rows = lax.broadcasted_iota(jnp.int16, (count, index_row.shape[1]), 0)
    return jnp.where(rows == index_row.astype(jnp.int16), BF(1.0), BF(0.0))


def row_update(embedding, accum, gradient):
    accum = accum + jnp.mean(gradient * gradient, axis=1, keepdims=True)
    return embedding - learn_rate * gradient / jnp.sqrt(accum), accum


def count_batch(idx_ref, member, base, rows, first, half):
    source = idx_ref[member, pl.ds(base, 1), :] - first
    target = idx_ref[member, pl.ds(base + 1, 1), :]
    relation = idx_ref[member, pl.ds(base + 2, 1), :]
    negative = idx_ref[member, pl.ds(base + 3, 1), :]
    pair = jnp.where((source >= 0) & (source < half), relation * half + source, -1)
    edges = dot(one_hot(target, rows), one_hot(pair, NREL * half), (1, 1))
    counts = dot(one_hot(negative, rows), jnp.ones((negative.shape[1], 128), BF), (1, 0))
    return edges, counts


def live_slots(idx_ref, bucket, nbatch):
    row = 8 * nbatch + bucket
    ends = [jnp.max(idx_ref[member, row : row + 1, :]) for member in range(idx_ref.shape[0])]
    for member in range(1, len(ends)):
        ends[member] = ends[member] + ends[member - 1]
    slots = []
    for slot in range(SLOTS):
        member, begin = jnp.int32(0), jnp.int32(0)
        for end in ends[:-1]:
            member = member + jnp.where(slot >= end, 1, 0)
            begin = jnp.where(slot >= end, end, begin)
        slots.append((member, (bucket * nbatch + jnp.minimum(slot - begin, nbatch - 1)) * 4))
    return ends[-1], slots


def score_grad(scores_t, edges_of, counts, total):
    for start in range(0, scores_t.shape[1], 128):
        cols = slice(start, start + 128)
        score = scores_t[:, cols]
        top = jnp.max(jnp.where(counts > 0.0, score, -3.0e38), axis=0, keepdims=True)
        above = score - top
        small = jnp.exp(-jnp.abs(above))
        weighted = counts * small
        neg_total = jnp.sum(weighted, axis=0, keepdims=True)
        neg_scale = jnp.where(above > 0.0, small, 1.0)
        pos_exp = jnp.where(above > 0.0, 1.0, small)
        factor = edges_of(cols) * neg_scale / (pos_exp + neg_total * neg_scale)
        factor_sum = jnp.sum(factor, axis=0, keepdims=True)
        total[:, cols] += weighted * factor_sum - neg_total * factor


def queries_and_scores(left_bf, right_bf, op_ref, query_t, scores_t):
    half = left_bf.shape[0]
    for r in range(NREL):
        cols = slice(r * half, (r + 1) * half)
        query_t[:, cols] = dot(op_ref[r].astype(BF), left_bf, (1, 1)).astype(BF)
    scores_t[...] = dot(right_bf, query_t[...], (1, 0))


def table_products(table_t, op_ref):
    half = table_t.shape[1] // NREL
    return sum(dot(table_t[:, r * half : (r + 1) * half], op_ref[r].astype(BF), (0, 0)) for r in range(NREL))


def operator_products(table_t, left_bf, r):
    half = left_bf.shape[0]
    return dot(table_t[:, r * half : (r + 1) * half], left_bf, (1, 0))


def pack_rows(out_ref, embedding, accum):
    half, width = embedding.shape
    out_ref[0:half, :] = embedding
    row = jnp.concatenate([to_row(accum)] * (width // half), axis=1)
    out_ref[half : half + 8, :] = jnp.broadcast_to(row, (8, width))


def gather_kernel(nbatch, *refs):
    sources, out_ref, buffers, sems = refs[:5], refs[5], refs[6:11], refs[11]
    copies = [pltpu.make_async_copy(a, b, sems.at[i]) for i, (a, b) in enumerate(zip(sources, buffers))]
    for copy in copies:
        copy.start()
    out_ref[8 * nbatch :, :] = jnp.zeros_like(out_ref[8 * nbatch :, :])
    for copy in copies:
        copy.wait()
    *buffers, live_ref = buffers
    for bucket in range(2):
        row = 8 * nbatch + bucket
        out_ref[row : row + 1, :] = jnp.full((1, out_ref.shape[1]), live_ref[0, 0, bucket])
    for bucket in range(2):
        for batch in range(nbatch):
            for i, buffer in enumerate(buffers):
                row = (bucket * nbatch + batch) * 4 + i
                out_ref[row : row + 1, :] = buffer[0, 0, bucket, batch : batch + 1, :]


def score_grads(live, scores_t, edges_ref, counts_ref, total):
    total[...] = jnp.zeros_like(total)

    def step(slot, _):
        score_grad(scores_t, lambda cols: edges_ref[slot, :, cols], counts_ref[slot], total)
        return 0

    lax.fori_loop(0, live, step, 0)


def first_kernel(
    nbatch, idx_ref, left_hbm, accum_hbm, right_hbm, op_hbm, left_out, query_t, grad_bf, table_t,
    left_ref, accum_ref, right_ref, op_ref, scores_t, total, edges_ref, counts_ref, sems
):
    rows, width = right_ref.shape
    half = left_ref.shape[0]
    first = pl.multiple_of(lax.axis_index("core") * half, half)
    pairs = (
        (op_hbm, op_ref),
        (left_hbm.at[pl.ds(first, half), :], left_ref),
        (right_hbm, right_ref),
        (accum_hbm, accum_ref),
    )
    copies = [pltpu.make_async_copy(*pair, sems.at[i]) for i, pair in enumerate(pairs)]
    for copy in copies:
        copy.start()
    live, slots = live_slots(idx_ref, 0, nbatch)
    for slot, (member, base) in enumerate(slots):
        edges_ref[slot], counts_ref[slot] = count_batch(idx_ref, member, base, rows, first, half)
    for copy in copies:
        copy.wait()
    right_bf = right_ref[...].astype(BF)
    queries_and_scores(left_ref[...].astype(BF), right_bf, op_ref, query_t, scores_t)
    score_grads(live, scores_t, edges_ref, counts_ref, total)
    grad_bf[...] = total[...].astype(BF)
    table_t[...] = dot(right_bf, grad_bf[...], (0, 0)).astype(BF)
    left_grad = table_products(table_t, op_ref)
    accum = to_column(accum_ref[:, pl.ds(first, half)])
    pack_rows(left_out, *row_update(left_ref[...], accum, left_grad))


def between_kernel(
    nbatch, idx_ref, left_ref, right_ref, accum_ref, op_ref, query_t, grad_bf, table_t,
    right_out, accum_out, grad_out, edges_out, counts_out,
    other_query_t, scores_t, total, edges_ref, counts_ref
):
    rows, width = right_ref.shape
    half = query_t.shape[1] // NREL
    core = lax.axis_index("core")
    mine = pl.multiple_of(core * half, half)
    other = pl.multiple_of((1 - core) * half, half)
    live, slots = live_slots(idx_ref, 0, nbatch)
    for slot, (member, base) in enumerate(slots):
        edges_ref[slot], counts_ref[slot] = count_batch(idx_ref, member, base, rows, other, half)
    right = right_ref[...]
    right_bf = right.astype(BF)
    left_bf = left_ref[pl.ds(other, half), :].astype(BF)
    queries_and_scores(left_bf, right_bf, op_ref, other_query_t, scores_t)
    _, slots = live_slots(idx_ref, 1, nbatch)
    for slot, (member, base) in enumerate(slots):
        edges_out[slot], counts_out[slot] = count_batch(idx_ref, member, base, rows, 0, rows)
    score_grads(live, scores_t, edges_ref, counts_ref, total)
    right_grad = dot(grad_bf[...], query_t[...], (1, 1)) + dot(total[...].astype(BF), other_query_t[...], (1, 1))
    right_out[...], accum = row_update(right, to_column(accum_ref[...]), right_grad)
    accum_out[...] = to_row(accum)
    cols = pl.ds(mine, half)
    other_table_t = dot(right_bf, total[:, cols].astype(BF), (0, 0)).astype(BF)
    my_left_bf = left_ref[pl.ds(mine, half), :].astype(BF)
    grad_out[...] = dot(table_t[:, cols], my_left_bf, (1, 0)) + dot(other_table_t, left_bf, (1, 0))


def second_kernel(
    nbatch, idx_ref, edges_ref, counts_ref, left_ref, right_ref, accum_ref, op_ref, grad_ref,
    left_out, left_accum_out, right_out, right_accum_out, grad_out, query_t, scores_t, total, grad_bf, table_t
):
    nrel = op_ref.shape[0]
    rows, width = right_ref.shape
    half = rows // 2
    left = jnp.concatenate([left_ref[0, 0:half, :], left_ref[1, 0:half, :]], axis=0)
    left_accum = jnp.concatenate([left_ref[0, half : half + 1, 0:half], left_ref[1, half : half + 1, 0:half]], axis=1)
    right = right_ref[...]
    left_bf, right_bf = left.astype(BF), right.astype(BF)
    queries_and_scores(left_bf, right_bf, op_ref, query_t, scores_t)
    live = 0
    for member in range(idx_ref.shape[0]):
        live += idx_ref[member, 8 * nbatch + 1 : 8 * nbatch + 2, :]
    score_grads(jnp.max(live), scores_t, edges_ref, counts_ref, total)
    grad_bf[...] = total[...].astype(BF)
    table_t[...] = dot(right_bf, grad_bf[...], (0, 0)).astype(BF)
    mine = pl.ds(pl.multiple_of(lax.axis_index("core") * rows, rows), rows)
    grad = dot(table_t[:, mine], left_bf, (1, 0)) + grad_ref[...]
    for part in range(2):
        grad_out[part] = grad[:, part * 128 : (part + 1) * 128].reshape(grad_out.shape[1:])
    left_grad = jnp.zeros((rows, width), F32)
    for r in range(nrel):
        left_grad += dot(table_t[:, r * rows : (r + 1) * rows], op_ref[r].astype(BF), (0, 0))
    left_out[...], accum = row_update(left, to_column(left_accum), left_grad)
    left_accum_out[...] = to_row(accum)
    right_grad = dot(grad_bf[...], query_t[...], (1, 1))
    right_out[...], accum = row_update(right, to_column(accum_ref[...]), right_grad)
    right_accum_out[...] = to_row(accum)


def final_kernel(total_ref, relation_ref, state_ref, relation_out, state_out):
    nrel, width, _ = relation_ref.shape
    for r in range(nrel):
        for part in range(2):
            cols = slice(part * 128, (part + 1) * 128)
            grad = total_ref[r, part].reshape(width, 128)
            state = state_ref[r, :, cols] + grad * grad
            state_out[r, :, cols] = state
            relation_out[r, :, cols] = relation_ref[r, :, cols] - learn_rate * grad / jnp.sqrt(state)


def f32(*shape):
    return jax.ShapeDtypeStruct(shape, F32)


def call(kernel, name, outs, args, scratch=(), flops=0, outside=()):
    spaces = [pltpu.HBM if i in outside else pltpu.VMEM for i in range(len(args))]
    sems = [pltpu.SemaphoreType.DMA((len(outside),))] if outside else []
    return pl.pallas_call(
        kernel,
        out_shape=outs,
        in_specs=[pl.BlockSpec(memory_space=space) for space in spaces],
        out_specs=[pl.BlockSpec(memory_space=pltpu.VMEM)] * len(outs),
        scratch_shapes=[pltpu.VMEM(*one) if isinstance(one, tuple) else one for one in scratch] + sems,
        compiler_params=pltpu.CompilerParams(vmem_limit_bytes=30 << 20),
        cost_estimate=pl.CostEstimate(flops=flops, bytes_accessed=4 << 20, transcendentals=0),
        name=name,
    )(*(pltpu.with_memory_space_constraint(a, pltpu.HBM) if i in outside else a for i, a in enumerate(args)))


def buckets(index, left, left_accum, right, right_accum, relation, nbatch, move):
    nrel, width, _ = relation.shape
    rows = left.shape[0]
    pairs = nrel * rows
    half = rows // 2
    mine = NREL * half
    bf16 = lambda *shape: jax.ShapeDtypeStruct(shape, BF)
    counts = [((SLOTS, rows, mine), F32), ((SLOTS, rows, 128), F32)]
    moved, query_t, grad_bf, table_t = call(
        functools.partial(first_kernel, nbatch),
        "bucket0_left",
        (f32(half + 8, width), bf16(width, mine), bf16(rows, mine), bf16(width, mine)),
        (index, left, left_accum, right, relation),
        [((half, width), F32), ((1, rows), F32), ((rows, width), F32), (relation.shape, F32),
         ((rows, mine), F32), ((rows, mine), F32), *counts],
        flops=2 << 30,
        outside=(1, 2, 3, 4),
    )
    moved = move(moved)
    right, right_accum, grad, edges, counts = call(
        functools.partial(between_kernel, nbatch),
        "bucket0_right",
        (f32(rows, width), f32(1, rows), f32(width, width), f32(SLOTS, rows, pairs), f32(SLOTS, rows, 128)),
        (index, left, right, right_accum, relation, query_t, grad_bf, table_t),
        [((width, mine), BF), ((rows, mine), F32), ((rows, mine), F32), *counts],
        flops=1 << 30,
    )
    moved = lax.all_gather(moved, "core", axis=0, tiled=False)
    return call(
        functools.partial(second_kernel, nbatch),
        "bucket1",
        (f32(rows, width), f32(1, rows), f32(rows, width), f32(1, rows), f32(2, width // 4, 4, 128)),
        (index, edges, counts, moved, right, right_accum, relation, grad),
        [((width, pairs), BF), ((rows, pairs), F32), ((rows, pairs), F32), ((rows, pairs), BF), ((width, pairs), BF)],
        flops=2 << 30,
    )


def body(
    left_emb,
    left_state,
    right_emb,
    right_state,
    relation,
    relation_state,
    edge_src,
    edge_dst,
    edge_rel,
    negatives,
    batch_counts,
):
    nbatch, batch = edge_src.shape[3:]
    rows, width = left_emb.shape
    blocks = lax.axis_size(BLK)
    index_rows = -(-(8 * nbatch + 2) // 8) * 8
    index = call(
        functools.partial(gather_kernel, nbatch),
        "gather_index",
        (jax.ShapeDtypeStruct((index_rows, batch), jnp.int32),),
        (edge_src, edge_dst, edge_rel, negatives, batch_counts),
        [(edge_src.shape, jnp.int32)] * 4 + [pltpu.SMEM(batch_counts.shape, jnp.int32)],
        outside=(0, 1, 2, 3, 4),
    )[0]
    index = lax.all_gather(index, REP, axis=0, tiled=False)
    route = [(i, (i + 1) % blocks) for i in range(blocks)]
    left, left_accum, right, right_accum, grad = buckets(
        index,
        left_emb,
        left_state.reshape(1, rows),
        right_emb,
        right_state.reshape(1, rows),
        relation,
        nbatch,
        lambda half: lax.ppermute(half, BLK, route),
    )
    grad = grad.reshape(blocks, -1, 128)
    grad = jnp.sum(lax.all_to_all(grad, BLK, 0, 0, tiled=True), axis=0)
    grad = jnp.broadcast_to(grad[None], (blocks, *grad.shape))
    grad = lax.all_to_all(grad, BLK, 0, 0, tiled=True)
    grad = lax.all_gather(grad, "core", axis=0, tiled=False)
    grad = grad.reshape(relation.shape[0], 2, width // 4, 4, 128)
    relation_new, relation_state_new = call(
        final_kernel, "final_update", (f32(*relation.shape),) * 2, (grad, relation, relation_state)
    )
    return (
        left,
        left_accum.reshape(rows),
        right,
        right_accum.reshape(rows),
        relation_new,
        relation_state_new,
    )


def solution(mesh):
    sizes = (8, 8, 2, 2, 2)
    mesh = jax.sharding.Mesh(mesh.devices.reshape(sizes), (*BLK, *REP))
    row, edge = P(BLK, None), P(BLK, REP, None, None, None)
    in_specs = (row, P(BLK), row, P(BLK), P(), P(), edge, edge, edge, edge, P(BLK, REP, None))
    out_specs = (row, P(BLK), row, P(BLK), P(), P())
    return jax.shard_map(body, mesh=mesh, in_specs=in_specs, out_specs=out_specs, check_vma=False)
```

```python
import functools

import jax
import jax.numpy as jnp
from jax import lax
from jax.experimental import pallas as pl
from jax.experimental.pallas import tpu as pltpu
from jax.sharding import PartitionSpec as P

learn_rate = 0.1
BF = jnp.bfloat16
F32 = jnp.float32
BLK = ("z", "y", "xl")
REP = ("xh", "core")
NREL = 2
SLOTS = 4


def dot(a, b, dims):
    return lax.dot_general(a, b, ((dims[:1], dims[1:]), ((), ())), preferred_element_type=F32)


def same(size):
    shape = (size, size)
    return lax.broadcasted_iota(jnp.int32, shape, 0) == lax.broadcasted_iota(jnp.int32, shape, 1)


def to_column(row):
    return jnp.sum(jnp.where(same(row.shape[1]), row, 0.0), axis=1, keepdims=True)


def to_row(column):
    return jnp.sum(jnp.where(same(column.shape[0]), column, 0.0), axis=0, keepdims=True)


def one_hot(index_row, count):
    rows = lax.broadcasted_iota(jnp.int16, (count, index_row.shape[1]), 0)
    return jnp.where(rows == index_row.astype(jnp.int16), BF(1.0), BF(0.0))


def row_update(embedding, accum, gradient):
    accum = accum + jnp.mean(gradient * gradient, axis=1, keepdims=True)
    return embedding - learn_rate * gradient / jnp.sqrt(accum), accum


def count_batch(idx_ref, member, base, rows, first, half):
    source = idx_ref[member, pl.ds(base, 1), :] - first
    target = idx_ref[member, pl.ds(base + 1, 1), :]
    relation = idx_ref[member, pl.ds(base + 2, 1), :]
    negative = idx_ref[member, pl.ds(base + 3, 1), :]
    pair = jnp.where((source >= 0) & (source < half), relation * half + source, -1)
    edges = dot(one_hot(target, rows), one_hot(pair, NREL * half), (1, 1))
    counts = dot(one_hot(negative, rows), jnp.ones((negative.shape[1], 128), BF), (1, 0))
    return edges, counts


def live_slots(idx_ref, bucket, nbatch):
    row = 8 * nbatch + bucket
    ends = [jnp.max(idx_ref[member, row : row + 1, :]) for member in range(idx_ref.shape[0])]
    for member in range(1, len(ends)):
        ends[member] = ends[member] + ends[member - 1]
    slots = []
    for slot in range(SLOTS):
        member, begin = jnp.int32(0), jnp.int32(0)
        for end in ends[:-1]:
            member = member + jnp.where(slot >= end, 1, 0)
            begin = jnp.where(slot >= end, end, begin)
        slots.append((member, (bucket * nbatch + jnp.minimum(slot - begin, nbatch - 1)) * 4))
    return ends[-1], slots


def score_grad(scores_t, edges_of, counts, total):
    absent = jnp.where(counts > 0.0, 0.0, -3.0e38)
    for start in range(0, scores_t.shape[1], 128):
        cols = slice(start, start + 128)
        score = scores_t[:, cols]
        top = jnp.max(score + absent, axis=0, keepdims=True)
        above = jnp.exp(jnp.minimum(score - top, 88.0))
        weighted = counts * above
        neg_total = jnp.sum(weighted, axis=0, keepdims=True)
        factor = edges_of(cols) / (above + neg_total)
        factor_sum = jnp.sum(factor, axis=0, keepdims=True)
        total[:, cols] += weighted * factor_sum - neg_total * factor


def queries_and_scores(left_bf, right_bf, op_ref, query_t, scores_t):
    half = left_bf.shape[0]
    for r in range(NREL):
        cols = slice(r * half, (r + 1) * half)
        query_t[:, cols] = dot(op_ref[r].astype(BF), left_bf, (1, 1)).astype(BF)
    scores_t[...] = dot(right_bf, query_t[...], (1, 0))


def table_products(table_t, op_ref):
    half = table_t.shape[1] // NREL
    return sum(dot(table_t[:, r * half : (r + 1) * half], op_ref[r].astype(BF), (0, 0)) for r in range(NREL))


def operator_products(table_t, left_bf, r):
    half = left_bf.shape[0]
    return dot(table_t[:, r * half : (r + 1) * half], left_bf, (1, 0))


def pack_rows(out_ref, embedding, accum):
    half, width = embedding.shape
    out_ref[0:half, :] = embedding
    row = jnp.concatenate([to_row(accum)] * (width // half), axis=1)
    out_ref[half : half + 8, :] = jnp.broadcast_to(row, (8, width))


def gather_kernel(nbatch, *refs):
    sources, out_ref, buffers, sems = refs[:5], refs[5], refs[6:11], refs[11]
    copies = [pltpu.make_async_copy(a, b, sems.at[i]) for i, (a, b) in enumerate(zip(sources, buffers))]
    for copy in copies:
        copy.start()
    out_ref[8 * nbatch :, :] = jnp.zeros_like(out_ref[8 * nbatch :, :])
    for copy in copies:
        copy.wait()
    *buffers, live_ref = buffers
    for bucket in range(2):
        row = 8 * nbatch + bucket
        out_ref[row : row + 1, :] = jnp.full((1, out_ref.shape[1]), live_ref[0, 0, bucket])
    for bucket in range(2):
        for batch in range(nbatch):
            for i, buffer in enumerate(buffers):
                row = (bucket * nbatch + batch) * 4 + i
                out_ref[row : row + 1, :] = buffer[0, 0, bucket, batch : batch + 1, :]


def score_grads(live, scores_t, edges_ref, counts_ref, total):
    total[...] = jnp.zeros_like(total)

    def step(slot, _):
        score_grad(scores_t, lambda cols: edges_ref[slot, :, cols], counts_ref[slot], total)
        return 0

    lax.fori_loop(0, live, step, 0)


def first_kernel(
    nbatch, idx_ref, left_hbm, accum_hbm, right_hbm, op_hbm, left_out, query_t, grad_bf, table_t,
    left_ref, accum_ref, right_ref, op_ref, scores_t, total, edges_ref, counts_ref, sems
):
    rows, width = right_ref.shape
    half = left_ref.shape[0]
    first = pl.multiple_of(lax.axis_index("core") * half, half)
    pairs = (
        (op_hbm, op_ref),
        (left_hbm.at[pl.ds(first, half), :], left_ref),
        (right_hbm, right_ref),
        (accum_hbm, accum_ref),
    )
    copies = [pltpu.make_async_copy(*pair, sems.at[i]) for i, pair in enumerate(pairs)]
    for copy in copies:
        copy.start()
    live, slots = live_slots(idx_ref, 0, nbatch)
    for slot, (member, base) in enumerate(slots):
        edges_ref[slot], counts_ref[slot] = count_batch(idx_ref, member, base, rows, first, half)
    for copy in copies:
        copy.wait()
    right_bf = right_ref[...].astype(BF)
    queries_and_scores(left_ref[...].astype(BF), right_bf, op_ref, query_t, scores_t)
    score_grads(live, scores_t, edges_ref, counts_ref, total)
    grad_bf[...] = total[...].astype(BF)
    table_t[...] = dot(right_bf, grad_bf[...], (0, 0)).astype(BF)
    left_grad = table_products(table_t, op_ref)
    accum = to_column(accum_ref[:, pl.ds(first, half)])
    pack_rows(left_out, *row_update(left_ref[...], accum, left_grad))


def between_kernel(
    nbatch, idx_ref, left_ref, right_ref, accum_ref, op_ref, query_t, grad_bf, table_t,
    right_out, accum_out, grad_out, edges_out, counts_out,
    other_query_t, scores_t, total, edges_ref, counts_ref
):
    rows, width = right_ref.shape
    half = query_t.shape[1] // NREL
    core = lax.axis_index("core")
    mine = pl.multiple_of(core * half, half)
    other = pl.multiple_of((1 - core) * half, half)
    live, slots = live_slots(idx_ref, 0, nbatch)
    for slot, (member, base) in enumerate(slots):
        edges_ref[slot], counts_ref[slot] = count_batch(idx_ref, member, base, rows, other, half)
    right = right_ref[...]
    right_bf = right.astype(BF)
    left_bf = left_ref[pl.ds(other, half), :].astype(BF)
    queries_and_scores(left_bf, right_bf, op_ref, other_query_t, scores_t)
    _, slots = live_slots(idx_ref, 1, nbatch)
    for slot, (member, base) in enumerate(slots):
        edges_out[slot], counts_out[slot] = count_batch(idx_ref, member, base, rows, 0, rows)
    score_grads(live, scores_t, edges_ref, counts_ref, total)
    right_grad = dot(grad_bf[...], query_t[...], (1, 1)) + dot(total[...].astype(BF), other_query_t[...], (1, 1))
    right_out[...], accum = row_update(right, to_column(accum_ref[...]), right_grad)
    accum_out[...] = to_row(accum)
    cols = pl.ds(mine, half)
    other_table_t = dot(right_bf, total[:, cols].astype(BF), (0, 0)).astype(BF)
    my_left_bf = left_ref[pl.ds(mine, half), :].astype(BF)
    grad_out[...] = dot(table_t[:, cols], my_left_bf, (1, 0)) + dot(other_table_t, left_bf, (1, 0))


def second_kernel(
    nbatch, idx_ref, edges_ref, counts_ref, left_ref, right_ref, accum_ref, op_ref, grad_ref,
    left_out, left_accum_out, right_out, right_accum_out, grad_out, query_t, scores_t, total, grad_bf, table_t
):
    nrel = op_ref.shape[0]
    rows, width = right_ref.shape
    half = rows // 2
    left = jnp.concatenate([left_ref[0, 0:half, :], left_ref[1, 0:half, :]], axis=0)
    left_accum = jnp.concatenate([left_ref[0, half : half + 1, 0:half], left_ref[1, half : half + 1, 0:half]], axis=1)
    right = right_ref[...]
    left_bf, right_bf = left.astype(BF), right.astype(BF)
    queries_and_scores(left_bf, right_bf, op_ref, query_t, scores_t)
    live = 0
    for member in range(idx_ref.shape[0]):
        live += idx_ref[member, 8 * nbatch + 1 : 8 * nbatch + 2, :]
    score_grads(jnp.max(live), scores_t, edges_ref, counts_ref, total)
    grad_bf[...] = total[...].astype(BF)
    table_t[...] = dot(right_bf, grad_bf[...], (0, 0)).astype(BF)
    mine = pl.ds(pl.multiple_of(lax.axis_index("core") * rows, rows), rows)
    grad = dot(table_t[:, mine], left_bf, (1, 0)) + grad_ref[...]
    for part in range(2):
        grad_out[part] = grad[:, part * 128 : (part + 1) * 128].reshape(grad_out.shape[1:])
    left_grad = jnp.zeros((rows, width), F32)
    for r in range(nrel):
        left_grad += dot(table_t[:, r * rows : (r + 1) * rows], op_ref[r].astype(BF), (0, 0))
    left_out[...], accum = row_update(left, to_column(left_accum), left_grad)
    left_accum_out[...] = to_row(accum)
    right_grad = dot(grad_bf[...], query_t[...], (1, 1))
    right_out[...], accum = row_update(right, to_column(accum_ref[...]), right_grad)
    right_accum_out[...] = to_row(accum)


def final_kernel(total_ref, relation_ref, state_ref, relation_out, state_out):
    nrel, width, _ = relation_ref.shape
    for r in range(nrel):
        for part in range(2):
            cols = slice(part * 128, (part + 1) * 128)
            grad = total_ref[r, part].reshape(width, 128)
            state = state_ref[r, :, cols] + grad * grad
            state_out[r, :, cols] = state
            relation_out[r, :, cols] = relation_ref[r, :, cols] - learn_rate * grad / jnp.sqrt(state)


def f32(*shape):
    return jax.ShapeDtypeStruct(shape, F32)


def call(kernel, name, outs, args, scratch=(), flops=0, outside=()):
    spaces = [pltpu.HBM if i in outside else pltpu.VMEM for i in range(len(args))]
    sems = [pltpu.SemaphoreType.DMA((len(outside),))] if outside else []
    return pl.pallas_call(
        kernel,
        out_shape=outs,
        in_specs=[pl.BlockSpec(memory_space=space) for space in spaces],
        out_specs=[pl.BlockSpec(memory_space=pltpu.VMEM)] * len(outs),
        scratch_shapes=[pltpu.VMEM(*one) if isinstance(one, tuple) else one for one in scratch] + sems,
        compiler_params=pltpu.CompilerParams(vmem_limit_bytes=30 << 20),
        cost_estimate=pl.CostEstimate(flops=flops, bytes_accessed=4 << 20, transcendentals=0),
        name=name,
    )(*(pltpu.with_memory_space_constraint(a, pltpu.HBM) if i in outside else a for i, a in enumerate(args)))


def buckets(index, left, left_accum, right, right_accum, relation, nbatch, move):
    nrel, width, _ = relation.shape
    rows = left.shape[0]
    pairs = nrel * rows
    half = rows // 2
    mine = NREL * half
    bf16 = lambda *shape: jax.ShapeDtypeStruct(shape, BF)
    counts = [((SLOTS, rows, mine), F32), ((SLOTS, rows, 128), F32)]
    moved, query_t, grad_bf, table_t = call(
        functools.partial(first_kernel, nbatch),
        "bucket0_left",
        (f32(half + 8, width), bf16(width, mine), bf16(rows, mine), bf16(width, mine)),
        (index, left, left_accum, right, relation),
        [((half, width), F32), ((1, rows), F32), ((rows, width), F32), (relation.shape, F32),
         ((rows, mine), F32), ((rows, mine), F32), *counts],
        flops=2 << 30,
        outside=(1, 2, 3, 4),
    )
    moved = move(moved)
    right, right_accum, grad, edges, counts = call(
        functools.partial(between_kernel, nbatch),
        "bucket0_right",
        (f32(rows, width), f32(1, rows), f32(width, width), f32(SLOTS, rows, pairs), f32(SLOTS, rows, 128)),
        (index, left, right, right_accum, relation, query_t, grad_bf, table_t),
        [((width, mine), BF), ((rows, mine), F32), ((rows, mine), F32), *counts],
        flops=1 << 30,
    )
    moved = lax.all_gather(moved, "core", axis=0, tiled=False)
    return call(
        functools.partial(second_kernel, nbatch),
        "bucket1",
        (f32(rows, width), f32(1, rows), f32(rows, width), f32(1, rows), f32(2, width // 4, 4, 128)),
        (index, edges, counts, moved, right, right_accum, relation, grad),
        [((width, pairs), BF), ((rows, pairs), F32), ((rows, pairs), F32), ((rows, pairs), BF), ((width, pairs), BF)],
        flops=2 << 30,
    )


def body(
    left_emb,
    left_state,
    right_emb,
    right_state,
    relation,
    relation_state,
    edge_src,
    edge_dst,
    edge_rel,
    negatives,
    batch_counts,
):
    nbatch, batch = edge_src.shape[3:]
    rows, width = left_emb.shape
    blocks = lax.axis_size(BLK)
    index_rows = -(-(8 * nbatch + 2) // 8) * 8
    index = call(
        functools.partial(gather_kernel, nbatch),
        "gather_index",
        (jax.ShapeDtypeStruct((index_rows, batch), jnp.int32),),
        (edge_src, edge_dst, edge_rel, negatives, batch_counts),
        [(edge_src.shape, jnp.int32)] * 4 + [pltpu.SMEM(batch_counts.shape, jnp.int32)],
        outside=(0, 1, 2, 3, 4),
    )[0]
    index = lax.all_gather(index, REP, axis=0, tiled=False)
    route = [(i, (i + 1) % blocks) for i in range(blocks)]
    left, left_accum, right, right_accum, grad = buckets(
        index,
        left_emb,
        left_state.reshape(1, rows),
        right_emb,
        right_state.reshape(1, rows),
        relation,
        nbatch,
        lambda half: lax.ppermute(half, BLK, route),
    )
    grad = grad.reshape(blocks, -1, 128)
    grad = jnp.sum(lax.all_to_all(grad, BLK, 0, 0, tiled=True), axis=0)
    grad = jnp.broadcast_to(grad[None], (blocks, *grad.shape))
    grad = lax.all_to_all(grad, BLK, 0, 0, tiled=True)
    grad = lax.all_gather(grad, "core", axis=0, tiled=False)
    grad = grad.reshape(relation.shape[0], 2, width // 4, 4, 128)
    relation_new, relation_state_new = call(
        final_kernel, "final_update", (f32(*relation.shape),) * 2, (grad, relation, relation_state)
    )
    return (
        left,
        left_accum.reshape(rows),
        right,
        right_accum.reshape(rows),
        relation_new,
        relation_state_new,
    )


def solution(mesh):
    sizes = (8, 8, 2, 2, 2)
    mesh = jax.sharding.Mesh(mesh.devices.reshape(sizes), (*BLK, *REP))
    row, edge = P(BLK, None), P(BLK, REP, None, None, None)
    in_specs = (row, P(BLK), row, P(BLK), P(), P(), edge, edge, edge, edge, P(BLK, REP, None))
    out_specs = (row, P(BLK), row, P(BLK), P(), P())
    return jax.shard_map(body, mesh=mesh, in_specs=in_specs, out_specs=out_specs, check_vma=False)
```

```python
import functools

import jax
import jax.numpy as jnp
from jax import lax
from jax.experimental import pallas as pl
from jax.experimental.pallas import tpu as pltpu
from jax.sharding import PartitionSpec as P

learn_rate = 0.1
BF = jnp.bfloat16
F32 = jnp.float32
BLK = ("z", "y", "xl")
REP = ("xh", "core")
NREL = 2
SLOTS = 4


def dot(a, b, dims):
    return lax.dot_general(a, b, ((dims[:1], dims[1:]), ((), ())), preferred_element_type=F32)


def same(size):
    shape = (size, size)
    return lax.broadcasted_iota(jnp.int32, shape, 0) == lax.broadcasted_iota(jnp.int32, shape, 1)


def to_column(row):
    return jnp.sum(jnp.where(same(row.shape[1]), row, 0.0), axis=1, keepdims=True)


def to_row(column):
    return jnp.sum(jnp.where(same(column.shape[0]), column, 0.0), axis=0, keepdims=True)


def one_hot(index_row, count):
    rows = lax.broadcasted_iota(jnp.int16, (count, index_row.shape[1]), 0)
    return jnp.where(rows == index_row.astype(jnp.int16), BF(1.0), BF(0.0))


def row_update(embedding, accum, gradient):
    accum = accum + jnp.mean(gradient * gradient, axis=1, keepdims=True)
    return embedding - learn_rate * gradient / jnp.sqrt(accum), accum


def count_batch(idx_ref, member, base, rows, first, half):
    source = idx_ref[member, pl.ds(base, 1), :] - first
    target = idx_ref[member, pl.ds(base + 1, 1), :]
    relation = idx_ref[member, pl.ds(base + 2, 1), :]
    negative = idx_ref[member, pl.ds(base + 3, 1), :]
    pair = jnp.where((source >= 0) & (source < half), relation * half + source, -1)
    edges = dot(one_hot(target, rows), one_hot(pair, NREL * half), (1, 1))
    counts = dot(one_hot(negative, rows), jnp.ones((negative.shape[1], 128), BF), (1, 0))
    return edges, counts


def live_slots(idx_ref, bucket, nbatch):
    row = 8 * nbatch + bucket
    ends = [jnp.max(idx_ref[member, row : row + 1, :]) for member in range(idx_ref.shape[0])]
    for member in range(1, len(ends)):
        ends[member] = ends[member] + ends[member - 1]
    slots = []
    for slot in range(SLOTS):
        member, begin = jnp.int32(0), jnp.int32(0)
        for end in ends[:-1]:
            member = member + jnp.where(slot >= end, 1, 0)
            begin = jnp.where(slot >= end, end, begin)
        slots.append((member, (bucket * nbatch + jnp.minimum(slot - begin, nbatch - 1)) * 4))
    return ends[-1], slots


def score_grad(scores_t, edges_of, counts, total):
    absent = jnp.where(counts > 0.0, 0.0, -3.0e38)
    for start in range(0, scores_t.shape[1], 128):
        cols = slice(start, start + 128)
        score = scores_t[:, cols]
        top = jnp.max(score + absent, axis=0, keepdims=True)
        above = jnp.exp(jnp.minimum(score - top, 88.0))
        weighted = counts * above
        neg_total = jnp.sum(weighted, axis=0, keepdims=True)
        factor = edges_of(cols) / (above + neg_total)
        factor_sum = jnp.sum(factor, axis=0, keepdims=True)
        total[:, cols] += weighted * factor_sum - neg_total * factor


def queries_and_scores(left_bf, right_bf, op_ref, query_t, scores_t):
    half = left_bf.shape[0]
    for r in range(NREL):
        cols = slice(r * half, (r + 1) * half)
        query_t[:, cols] = dot(op_ref[r].astype(BF), left_bf, (1, 1)).astype(BF)
    scores_t[...] = dot(right_bf, query_t[...], (1, 0))


def table_products(table_t, op_ref):
    half = table_t.shape[1] // NREL
    return sum(dot(table_t[:, r * half : (r + 1) * half], op_ref[r].astype(BF), (0, 0)) for r in range(NREL))


def operator_products(table_t, left_bf, r):
    half = left_bf.shape[0]
    return dot(table_t[:, r * half : (r + 1) * half], left_bf, (1, 0))


def pack_rows(out_ref, embedding, accum):
    half, width = embedding.shape
    out_ref[0:half, :] = embedding
    row = jnp.concatenate([to_row(accum)] * (width // half), axis=1)
    out_ref[half : half + 8, :] = jnp.broadcast_to(row, (8, width))


def gather_kernel(nbatch, *refs):
    sources, staged, out_ref = refs[:5], refs[5:10], refs[10]
    held, buffers, sems = refs[11:16], refs[16:21], refs[21]
    pairs = [*zip(sources, buffers), *zip(staged, held)]
    copies = [pltpu.make_async_copy(*pair, sems.at[i]) for i, pair in enumerate(pairs)]
    for copy in copies:
        copy.start()
    out_ref[8 * nbatch :, :] = jnp.zeros_like(out_ref[8 * nbatch :, :])
    for copy in copies[: len(sources)]:
        copy.wait()
    *buffers, live_ref = buffers
    for bucket in range(2):
        row = 8 * nbatch + bucket
        out_ref[row : row + 1, :] = jnp.full((1, out_ref.shape[1]), live_ref[0, 0, bucket])
    for bucket in range(2):
        for batch in range(nbatch):
            for i, buffer in enumerate(buffers):
                row = (bucket * nbatch + batch) * 4 + i
                out_ref[row : row + 1, :] = buffer[0, 0, bucket, batch : batch + 1, :]
    for copy in copies[len(sources) :]:
        copy.wait()


def score_grads(live, scores_t, edges_ref, counts_ref, total):
    total[...] = jnp.zeros_like(total)

    def step(slot, _):
        score_grad(scores_t, lambda cols: edges_ref[slot, :, cols], counts_ref[slot], total)
        return 0

    lax.fori_loop(0, live, step, 0)


def first_kernel(
    nbatch, idx_ref, left_all_ref, accum_ref, right_ref, op_ref, left_out, query_t, grad_bf, table_t,
    scores_t, total, edges_ref, counts_ref
):
    rows, width = right_ref.shape
    half = rows // 2
    first = pl.multiple_of(lax.axis_index("core") * half, half)
    left = left_all_ref[pl.ds(first, half), :]
    live, slots = live_slots(idx_ref, 0, nbatch)
    for slot, (member, base) in enumerate(slots):
        edges_ref[slot], counts_ref[slot] = count_batch(idx_ref, member, base, rows, first, half)
    right_bf = right_ref[...].astype(BF)
    queries_and_scores(left.astype(BF), right_bf, op_ref, query_t, scores_t)
    score_grads(live, scores_t, edges_ref, counts_ref, total)
    grad_bf[...] = total[...].astype(BF)
    table_t[...] = dot(right_bf, grad_bf[...], (0, 0)).astype(BF)
    left_grad = table_products(table_t, op_ref)
    accum = to_column(accum_ref[:, pl.ds(first, half)])
    pack_rows(left_out, *row_update(left, accum, left_grad))


def between_kernel(
    nbatch, idx_ref, left_ref, right_ref, accum_ref, op_ref, query_t, grad_bf, table_t,
    right_out, accum_out, grad_out, edges_out, counts_out,
    other_query_t, scores_t, total, edges_ref, counts_ref
):
    rows, width = right_ref.shape
    half = query_t.shape[1] // NREL
    core = lax.axis_index("core")
    mine = pl.multiple_of(core * half, half)
    other = pl.multiple_of((1 - core) * half, half)
    live, slots = live_slots(idx_ref, 0, nbatch)
    for slot, (member, base) in enumerate(slots):
        edges_ref[slot], counts_ref[slot] = count_batch(idx_ref, member, base, rows, other, half)
    right = right_ref[...]
    right_bf = right.astype(BF)
    left_bf = left_ref[pl.ds(other, half), :].astype(BF)
    queries_and_scores(left_bf, right_bf, op_ref, other_query_t, scores_t)
    _, slots = live_slots(idx_ref, 1, nbatch)
    for slot, (member, base) in enumerate(slots):
        edges_out[slot], counts_out[slot] = count_batch(idx_ref, member, base, rows, 0, rows)
    score_grads(live, scores_t, edges_ref, counts_ref, total)
    right_grad = dot(grad_bf[...], query_t[...], (1, 1)) + dot(total[...].astype(BF), other_query_t[...], (1, 1))
    right_out[...], accum = row_update(right, to_column(accum_ref[...]), right_grad)
    accum_out[...] = to_row(accum)
    cols = pl.ds(mine, half)
    other_table_t = dot(right_bf, total[:, cols].astype(BF), (0, 0)).astype(BF)
    my_left_bf = left_ref[pl.ds(mine, half), :].astype(BF)
    grad_out[...] = dot(table_t[:, cols], my_left_bf, (1, 0)) + dot(other_table_t, left_bf, (1, 0))


def second_kernel(
    nbatch, idx_ref, edges_ref, counts_ref, left_ref, right_ref, accum_ref, op_ref, grad_ref,
    left_out, left_accum_out, right_out, right_accum_out, grad_out, query_t, scores_t, total, grad_bf, table_t
):
    nrel = op_ref.shape[0]
    rows, width = right_ref.shape
    half = rows // 2
    left = jnp.concatenate([left_ref[0, 0:half, :], left_ref[1, 0:half, :]], axis=0)
    left_accum = jnp.concatenate([left_ref[0, half : half + 1, 0:half], left_ref[1, half : half + 1, 0:half]], axis=1)
    right = right_ref[...]
    left_bf, right_bf = left.astype(BF), right.astype(BF)
    queries_and_scores(left_bf, right_bf, op_ref, query_t, scores_t)
    live = 0
    for member in range(idx_ref.shape[0]):
        live += idx_ref[member, 8 * nbatch + 1 : 8 * nbatch + 2, :]
    score_grads(jnp.max(live), scores_t, edges_ref, counts_ref, total)
    grad_bf[...] = total[...].astype(BF)
    table_t[...] = dot(right_bf, grad_bf[...], (0, 0)).astype(BF)
    mine = pl.ds(pl.multiple_of(lax.axis_index("core") * rows, rows), rows)
    grad = dot(table_t[:, mine], left_bf, (1, 0)) + grad_ref[...]
    for part in range(2):
        grad_out[part] = grad[:, part * 128 : (part + 1) * 128].reshape(grad_out.shape[1:])
    left_grad = jnp.zeros((rows, width), F32)
    for r in range(nrel):
        left_grad += dot(table_t[:, r * rows : (r + 1) * rows], op_ref[r].astype(BF), (0, 0))
    left_out[...], accum = row_update(left, to_column(left_accum), left_grad)
    left_accum_out[...] = to_row(accum)
    right_grad = dot(grad_bf[...], query_t[...], (1, 1))
    right_out[...], accum = row_update(right, to_column(accum_ref[...]), right_grad)
    right_accum_out[...] = to_row(accum)


def final_kernel(total_ref, relation_ref, state_ref, relation_out, state_out):
    nrel, width, _ = relation_ref.shape
    for r in range(nrel):
        for part in range(2):
            cols = slice(part * 128, (part + 1) * 128)
            grad = total_ref[r, part].reshape(width, 128)
            state = state_ref[r, :, cols] + grad * grad
            state_out[r, :, cols] = state
            relation_out[r, :, cols] = relation_ref[r, :, cols] - learn_rate * grad / jnp.sqrt(state)


def f32(*shape):
    return jax.ShapeDtypeStruct(shape, F32)


def call(kernel, name, outs, args, scratch=(), flops=0, outside=()):
    spaces = [pltpu.HBM if i in outside else pltpu.VMEM for i in range(len(args))]
    sems = [pltpu.SemaphoreType.DMA((len(outside),))] if outside else []
    return pl.pallas_call(
        kernel,
        out_shape=outs,
        in_specs=[pl.BlockSpec(memory_space=space) for space in spaces],
        out_specs=[pl.BlockSpec(memory_space=pltpu.VMEM)] * len(outs),
        scratch_shapes=[pltpu.VMEM(*one) if isinstance(one, tuple) else one for one in scratch] + sems,
        compiler_params=pltpu.CompilerParams(vmem_limit_bytes=30 << 20),
        cost_estimate=pl.CostEstimate(flops=flops, bytes_accessed=4 << 20, transcendentals=0),
        name=name,
    )(*(pltpu.with_memory_space_constraint(a, pltpu.HBM) if i in outside else a for i, a in enumerate(args)))


def buckets(index, left, left_accum, right, right_accum, relation, nbatch, move):
    nrel, width, _ = relation.shape
    rows = left.shape[0]
    pairs = nrel * rows
    half = rows // 2
    mine = NREL * half
    bf16 = lambda *shape: jax.ShapeDtypeStruct(shape, BF)
    counts = [((SLOTS, rows, mine), F32), ((SLOTS, rows, 128), F32)]
    moved, query_t, grad_bf, table_t = call(
        functools.partial(first_kernel, nbatch),
        "bucket0_left",
        (f32(half + 8, width), bf16(width, mine), bf16(rows, mine), bf16(width, mine)),
        (index, left, left_accum, right, relation),
        [((rows, mine), F32), ((rows, mine), F32), *counts],
        flops=2 << 30,
    )
    moved = move(moved)
    right, right_accum, grad, edges, counts = call(
        functools.partial(between_kernel, nbatch),
        "bucket0_right",
        (f32(rows, width), f32(1, rows), f32(width, width), f32(SLOTS, rows, pairs), f32(SLOTS, rows, 128)),
        (index, left, right, right_accum, relation, query_t, grad_bf, table_t),
        [((width, mine), BF), ((rows, mine), F32), ((rows, mine), F32), *counts],
        flops=1 << 30,
    )
    moved = lax.all_gather(moved, "core", axis=0, tiled=False)
    return call(
        functools.partial(second_kernel, nbatch),
        "bucket1",
        (f32(rows, width), f32(1, rows), f32(rows, width), f32(1, rows), f32(2, width // 4, 4, 128)),
        (index, edges, counts, moved, right, right_accum, relation, grad),
        [((width, pairs), BF), ((rows, pairs), F32), ((rows, pairs), F32), ((rows, pairs), BF), ((width, pairs), BF)],
        flops=2 << 30,
    )


def body(
    left_emb,
    left_state,
    right_emb,
    right_state,
    relation,
    relation_state,
    edge_src,
    edge_dst,
    edge_rel,
    negatives,
    batch_counts,
):
    nbatch, batch = edge_src.shape[3:]
    rows, width = left_emb.shape
    blocks = lax.axis_size(BLK)
    index_rows = -(-(8 * nbatch + 2) // 8) * 8
    arrays = (left_emb, left_state.reshape(1, rows), right_emb, right_state.reshape(1, rows), relation)
    index, *arrays = call(
        functools.partial(gather_kernel, nbatch),
        "gather_index",
        (jax.ShapeDtypeStruct((index_rows, batch), jnp.int32), *(f32(*array.shape) for array in arrays)),
        (edge_src, edge_dst, edge_rel, negatives, batch_counts, *arrays),
        [(edge_src.shape, jnp.int32)] * 4 + [pltpu.SMEM(batch_counts.shape, jnp.int32)],
        outside=tuple(range(10)),
    )
    index = lax.all_gather(index, REP, axis=0, tiled=False)
    route = [(i, (i + 1) % blocks) for i in range(blocks)]
    left, left_accum, right, right_accum, grad = buckets(
        index,
        *arrays,
        nbatch,
        lambda half: lax.ppermute(half, BLK, route),
    )
    grad = grad.reshape(blocks, -1, 128)
    grad = jnp.sum(lax.all_to_all(grad, BLK, 0, 0, tiled=True), axis=0)
    grad = jnp.broadcast_to(grad[None], (blocks, *grad.shape))
    grad = lax.all_to_all(grad, BLK, 0, 0, tiled=True)
    grad = lax.all_gather(grad, "core", axis=0, tiled=False)
    grad = grad.reshape(relation.shape[0], 2, width // 4, 4, 128)
    relation_new, relation_state_new = call(
        final_kernel, "final_update", (f32(*relation.shape),) * 2, (grad, arrays[-1], relation_state)
    )
    return (
        left,
        left_accum.reshape(rows),
        right,
        right_accum.reshape(rows),
        relation_new,
        relation_state_new,
    )


def solution(mesh):
    sizes = (8, 8, 2, 2, 2)
    mesh = jax.sharding.Mesh(mesh.devices.reshape(sizes), (*BLK, *REP))
    row, edge = P(BLK, None), P(BLK, REP, None, None, None)
    in_specs = (row, P(BLK), row, P(BLK), P(), P(), edge, edge, edge, edge, P(BLK, REP, None))
    out_specs = (row, P(BLK), row, P(BLK), P(), P())
    return jax.shard_map(body, mesh=mesh, in_specs=in_specs, out_specs=out_specs, check_vma=False)
```

```python
import functools

import jax
import jax.numpy as jnp
from jax import lax
from jax.experimental import pallas as pl
from jax.experimental.pallas import tpu as pltpu
from jax.sharding import PartitionSpec as P

learn_rate = 0.1
BF = jnp.bfloat16
F32 = jnp.float32
BLK = ("z", "y", "xl")
REP = ("xh", "core")
NREL = 2
LANES = 128
SLOTS = 4


def dot(a, b, dims):
    return lax.dot_general(a, b, ((dims[:1], dims[1:]), ((), ())), preferred_element_type=F32)


def same(size):
    shape = (size, size)
    return lax.broadcasted_iota(jnp.int32, shape, 0) == lax.broadcasted_iota(jnp.int32, shape, 1)


def to_column(row):
    return jnp.sum(jnp.where(same(row.shape[1]), row, 0.0), axis=1, keepdims=True)


def to_row(column):
    return jnp.sum(jnp.where(same(column.shape[0]), column, 0.0), axis=0, keepdims=True)


def one_hot(index_row, count):
    rows = lax.broadcasted_iota(jnp.int16, (count, index_row.shape[1]), 0)
    return jnp.where(rows == index_row.astype(jnp.int16), BF(1.0), BF(0.0))


def row_update(embedding, accum, gradient):
    accum = accum + jnp.mean(gradient * gradient, axis=1, keepdims=True)
    return embedding - learn_rate * gradient / jnp.sqrt(accum), accum


def count_batch(idx_ref, live, member, base, rows, first, half):
    source = idx_ref[member, pl.ds(base, 1), :] - first
    target = idx_ref[member, pl.ds(base + 1, 1), :]
    relation = idx_ref[member, pl.ds(base + 2, 1), :]
    negative = idx_ref[member, pl.ds(base + 3, 1), :]
    pair = jnp.where((source >= 0) & (source < half) & live, relation * half + source, -1)
    edges = dot(one_hot(target, rows), one_hot(pair, NREL * half), (1, 1))
    counts = dot(one_hot(negative, rows), jnp.ones((negative.shape[1], LANES), BF), (1, 0))
    return edges, jnp.stack([counts, jnp.where(counts > 0.0, 0.0, -3.0e38)])


def live_slots(idx_ref, bucket, nbatch):
    row = 8 * nbatch + bucket
    ends = [jnp.max(idx_ref[member, row : row + 1, :]) for member in range(idx_ref.shape[0])]
    for member in range(1, len(ends)):
        ends[member] = ends[member] + ends[member - 1]
    slots = []
    for slot in range(SLOTS):
        member, begin = jnp.int32(0), jnp.int32(0)
        for end in ends[:-1]:
            member = member + jnp.where(slot >= end, 1, 0)
            begin = jnp.where(slot >= end, end, begin)
        slots.append((slot < ends[-1], member, (bucket * nbatch + jnp.minimum(slot - begin, nbatch - 1)) * 4))
    return slots


def score_grads(scores_t, edges_ref, counts_ref, grad_bf):
    for start in range(0, scores_t.shape[1], LANES):
        cols = slice(start, start + LANES)
        score = scores_t[:, cols]
        total = 0.0
        for slot in range(SLOTS):
            counts = counts_ref[slot, 0]
            top = jnp.max(score + counts_ref[slot, 1], axis=0, keepdims=True)
            above = jnp.exp(jnp.minimum(score - top, 88.0))
            weighted = counts * above
            neg_total = jnp.sum(weighted, axis=0, keepdims=True)
            factor = edges_ref[slot, :, cols] / (above + neg_total)
            factor_sum = jnp.sum(factor, axis=0, keepdims=True)
            total += weighted * factor_sum - neg_total * factor
        grad_bf[:, cols] = total.astype(BF)


def queries_and_scores(left_bf, right_bf, op_ref, query_t, scores_t):
    half = left_bf.shape[0]
    for r in range(NREL):
        cols = slice(r * half, (r + 1) * half)
        query_t[:, cols] = dot(op_ref[r].astype(BF), left_bf, (1, 1)).astype(BF)
    scores_t[...] = dot(right_bf, query_t[...], (1, 0))


def table_products(table_t, op_ref):
    half = table_t.shape[1] // NREL
    return sum(dot(table_t[:, r * half : (r + 1) * half], op_ref[r].astype(BF), (0, 0)) for r in range(NREL))


def operator_products(table_t, left_bf, r):
    half = left_bf.shape[0]
    return dot(table_t[:, r * half : (r + 1) * half], left_bf, (1, 0))


def pack_rows(out_ref, embedding, accum):
    half, width = embedding.shape
    out_ref[0:half, :] = embedding
    row = jnp.concatenate([to_row(accum)] * (width // half), axis=1)
    out_ref[half : half + 8, :] = jnp.broadcast_to(row, (8, width))


def gather_kernel(nbatch, *refs):
    sources, staged, out_ref = refs[:5], refs[5:10], refs[10]
    held, buffers, sems = refs[11:16], refs[16:21], refs[21]
    pairs = [*zip(sources, buffers), *zip(staged, held)]
    copies = [pltpu.make_async_copy(*pair, sems.at[i]) for i, pair in enumerate(pairs)]
    for copy in copies:
        copy.start()
    out_ref[8 * nbatch :, :] = jnp.zeros_like(out_ref[8 * nbatch :, :])
    for copy in copies[: len(sources)]:
        copy.wait()
    *buffers, live_ref = buffers
    for bucket in range(2):
        row = 8 * nbatch + bucket
        out_ref[row : row + 1, :] = jnp.full((1, out_ref.shape[1]), live_ref[0, 0, bucket])
    for bucket in range(2):
        for batch in range(nbatch):
            for i, buffer in enumerate(buffers):
                row = (bucket * nbatch + batch) * 4 + i
                out_ref[row : row + 1, :] = buffer[0, 0, bucket, batch : batch + 1, :]
    for copy in copies[len(sources) :]:
        copy.wait()


def first_kernel(
    nbatch, idx_ref, left_all_ref, accum_ref, right_ref, op_ref, left_out, query_t, grad_bf, table_t,
    scores_t, edges_ref, counts_ref
):
    rows, width = right_ref.shape
    half = rows // 2
    first = pl.multiple_of(lax.axis_index("core") * half, half)
    left = left_all_ref[pl.ds(first, half), :]
    slots = live_slots(idx_ref, 0, nbatch)
    for slot, batch in enumerate(slots):
        edges_ref[slot], counts_ref[slot] = count_batch(idx_ref, *batch, rows, first, half)
    right_bf = right_ref[...].astype(BF)
    queries_and_scores(left.astype(BF), right_bf, op_ref, query_t, scores_t)
    score_grads(scores_t, edges_ref, counts_ref, grad_bf)
    table_t[...] = dot(right_bf, grad_bf[...], (0, 0)).astype(BF)
    left_grad = table_products(table_t, op_ref)
    accum = to_column(accum_ref[:, pl.ds(first, half)])
    pack_rows(left_out, *row_update(left, accum, left_grad))


def between_kernel(
    nbatch, idx_ref, left_ref, right_ref, accum_ref, op_ref, query_t, grad_bf, table_t,
    right_out, accum_out, grad_out, edges_out, counts_out,
    other_query_t, scores_t, other_grad_bf, edges_ref, counts_ref
):
    rows, width = right_ref.shape
    half = query_t.shape[1] // NREL
    core = lax.axis_index("core")
    mine = pl.multiple_of(core * half, half)
    other = pl.multiple_of((1 - core) * half, half)
    slots = live_slots(idx_ref, 0, nbatch)
    for slot, batch in enumerate(slots):
        edges_ref[slot], counts_ref[slot] = count_batch(idx_ref, *batch, rows, other, half)
    right = right_ref[...]
    right_bf = right.astype(BF)
    left_bf = left_ref[pl.ds(other, half), :].astype(BF)
    queries_and_scores(left_bf, right_bf, op_ref, other_query_t, scores_t)
    slots = live_slots(idx_ref, 1, nbatch)
    for slot, batch in enumerate(slots):
        edges_out[slot], counts_out[slot] = count_batch(idx_ref, *batch, rows, 0, rows)
    score_grads(scores_t, edges_ref, counts_ref, other_grad_bf)
    right_grad = dot(grad_bf[...], query_t[...], (1, 1)) + dot(other_grad_bf[...], other_query_t[...], (1, 1))
    right_out[...], accum = row_update(right, to_column(accum_ref[...]), right_grad)
    accum_out[...] = to_row(accum)
    cols = pl.ds(mine, half)
    other_table_t = dot(right_bf, other_grad_bf[:, cols], (0, 0)).astype(BF)
    my_left_bf = left_ref[pl.ds(mine, half), :].astype(BF)
    grad_out[...] = dot(table_t[:, cols], my_left_bf, (1, 0)) + dot(other_table_t, left_bf, (1, 0))


def second_kernel(
    edges_ref, counts_ref, left_ref, right_ref, accum_ref, op_ref, grad_ref,
    left_out, left_accum_out, right_out, right_accum_out, grad_out, query_t, scores_t, grad_bf, table_t
):
    nrel = op_ref.shape[0]
    rows, width = right_ref.shape
    half = rows // 2
    left = jnp.concatenate([left_ref[0, 0:half, :], left_ref[1, 0:half, :]], axis=0)
    left_accum = jnp.concatenate([left_ref[0, half : half + 1, 0:half], left_ref[1, half : half + 1, 0:half]], axis=1)
    right = right_ref[...]
    left_bf, right_bf = left.astype(BF), right.astype(BF)
    queries_and_scores(left_bf, right_bf, op_ref, query_t, scores_t)
    score_grads(scores_t, edges_ref, counts_ref, grad_bf)
    table_t[...] = dot(right_bf, grad_bf[...], (0, 0)).astype(BF)
    mine = pl.ds(pl.multiple_of(lax.axis_index("core") * rows, rows), rows)
    grad = dot(table_t[:, mine], left_bf, (1, 0)) + grad_ref[...]
    for part in range(2):
        grad_out[part] = grad[:, part * 128 : (part + 1) * 128].reshape(grad_out.shape[1:])
    left_grad = jnp.zeros((rows, width), F32)
    for r in range(nrel):
        left_grad += dot(table_t[:, r * rows : (r + 1) * rows], op_ref[r].astype(BF), (0, 0))
    left_out[...], accum = row_update(left, to_column(left_accum), left_grad)
    left_accum_out[...] = to_row(accum)
    right_grad = dot(grad_bf[...], query_t[...], (1, 1))
    right_out[...], accum = row_update(right, to_column(accum_ref[...]), right_grad)
    right_accum_out[...] = to_row(accum)


def final_kernel(total_ref, relation_ref, state_ref, relation_out, state_out):
    nrel, width, _ = relation_ref.shape
    for r in range(nrel):
        for part in range(2):
            cols = slice(part * 128, (part + 1) * 128)
            grad = total_ref[r, part].reshape(width, 128)
            state = state_ref[r, :, cols] + grad * grad
            state_out[r, :, cols] = state
            relation_out[r, :, cols] = relation_ref[r, :, cols] - learn_rate * grad / jnp.sqrt(state)


def f32(*shape):
    return jax.ShapeDtypeStruct(shape, F32)


def call(kernel, name, outs, args, scratch=(), flops=0, outside=()):
    spaces = [pltpu.HBM if i in outside else pltpu.VMEM for i in range(len(args))]
    sems = [pltpu.SemaphoreType.DMA((len(outside),))] if outside else []
    return pl.pallas_call(
        kernel,
        out_shape=outs,
        in_specs=[pl.BlockSpec(memory_space=space) for space in spaces],
        out_specs=[pl.BlockSpec(memory_space=pltpu.VMEM)] * len(outs),
        scratch_shapes=[pltpu.VMEM(*one) if isinstance(one, tuple) else one for one in scratch] + sems,
        compiler_params=pltpu.CompilerParams(vmem_limit_bytes=30 << 20),
        cost_estimate=pl.CostEstimate(flops=flops, bytes_accessed=4 << 20, transcendentals=0),
        name=name,
    )(*(pltpu.with_memory_space_constraint(a, pltpu.HBM) if i in outside else a for i, a in enumerate(args)))


def buckets(index, left, left_accum, right, right_accum, relation, nbatch, move):
    nrel, width, _ = relation.shape
    rows = left.shape[0]
    pairs = nrel * rows
    half = rows // 2
    mine = NREL * half
    bf16 = lambda *shape: jax.ShapeDtypeStruct(shape, BF)
    counts = [((SLOTS, rows, mine), F32), ((SLOTS, 2, rows, LANES), F32)]
    moved, query_t, grad_bf, table_t = call(
        functools.partial(first_kernel, nbatch),
        "bucket0_left",
        (f32(half + 8, width), bf16(width, mine), bf16(rows, mine), bf16(width, mine)),
        (index, left, left_accum, right, relation),
        [((rows, mine), F32), *counts],
        flops=2 << 30,
    )
    moved = move(moved)
    right, right_accum, grad, edges, counts = call(
        functools.partial(between_kernel, nbatch),
        "bucket0_right",
        (f32(rows, width), f32(1, rows), f32(width, width), f32(SLOTS, rows, pairs), f32(SLOTS, 2, rows, LANES)),
        (index, left, right, right_accum, relation, query_t, grad_bf, table_t),
        [((width, mine), BF), ((rows, mine), F32), ((rows, mine), BF), *counts],
        flops=1 << 30,
    )
    moved = lax.all_gather(moved, "core", axis=0, tiled=False)
    return call(
        second_kernel,
        "bucket1",
        (f32(rows, width), f32(1, rows), f32(rows, width), f32(1, rows), f32(2, width // 4, 4, 128)),
        (edges, counts, moved, right, right_accum, relation, grad),
        [((width, pairs), BF), ((rows, pairs), F32), ((rows, pairs), BF), ((width, pairs), BF)],
        flops=2 << 30,
    )


def body(
    left_emb,
    left_state,
    right_emb,
    right_state,
    relation,
    relation_state,
    edge_src,
    edge_dst,
    edge_rel,
    negatives,
    batch_counts,
):
    nbatch, batch = edge_src.shape[3:]
    rows, width = left_emb.shape
    blocks = lax.axis_size(BLK)
    index_rows = -(-(8 * nbatch + 2) // 8) * 8
    arrays = (left_emb, left_state.reshape(1, rows), right_emb, right_state.reshape(1, rows), relation)
    index, *arrays = call(
        functools.partial(gather_kernel, nbatch),
        "gather_index",
        (jax.ShapeDtypeStruct((index_rows, batch), jnp.int32), *(f32(*array.shape) for array in arrays)),
        (edge_src, edge_dst, edge_rel, negatives, batch_counts, *arrays),
        [(edge_src.shape, jnp.int32)] * 4 + [pltpu.SMEM(batch_counts.shape, jnp.int32)],
        outside=tuple(range(10)),
    )
    index = lax.all_gather(index, REP, axis=0, tiled=False)
    route = [(i, (i + 1) % blocks) for i in range(blocks)]
    left, left_accum, right, right_accum, grad = buckets(
        index,
        *arrays,
        nbatch,
        lambda half: lax.ppermute(half, BLK, route),
    )
    grad = grad.reshape(blocks, -1, 128)
    grad = jnp.sum(lax.all_to_all(grad, BLK, 0, 0, tiled=True), axis=0)
    grad = jnp.broadcast_to(grad[None], (blocks, *grad.shape))
    grad = lax.all_to_all(grad, BLK, 0, 0, tiled=True)
    grad = lax.all_gather(grad, "core", axis=0, tiled=False)
    grad = grad.reshape(relation.shape[0], 2, width // 4, 4, 128)
    relation_new, relation_state_new = call(
        final_kernel, "final_update", (f32(*relation.shape),) * 2, (grad, arrays[-1], relation_state)
    )
    return (
        left,
        left_accum.reshape(rows),
        right,
        right_accum.reshape(rows),
        relation_new,
        relation_state_new,
    )


def solution(mesh):
    sizes = (8, 8, 2, 2, 2)
    mesh = jax.sharding.Mesh(mesh.devices.reshape(sizes), (*BLK, *REP))
    row, edge = P(BLK, None), P(BLK, REP, None, None, None)
    in_specs = (row, P(BLK), row, P(BLK), P(), P(), edge, edge, edge, edge, P(BLK, REP, None))
    out_specs = (row, P(BLK), row, P(BLK), P(), P())
    return jax.shard_map(body, mesh=mesh, in_specs=in_specs, out_specs=out_specs, check_vma=False)
```

```python
import functools

import jax
import jax.numpy as jnp
from jax import lax
from jax.experimental import pallas as pl
from jax.experimental.pallas import tpu as pltpu
from jax.sharding import PartitionSpec as P

learn_rate = 0.1
BF = jnp.bfloat16
F32 = jnp.float32
BLK = ("z", "y", "xl")
REP = ("xh", "core")
NREL = 2
LANES = 128
SLOTS = 4


def dot(a, b, dims):
    return lax.dot_general(a, b, ((dims[:1], dims[1:]), ((), ())), preferred_element_type=F32)


def same(size):
    shape = (size, size)
    return lax.broadcasted_iota(jnp.int32, shape, 0) == lax.broadcasted_iota(jnp.int32, shape, 1)


def to_column(row):
    return jnp.sum(jnp.where(same(row.shape[1]), row, 0.0), axis=1, keepdims=True)


def to_row(column):
    return jnp.sum(jnp.where(same(column.shape[0]), column, 0.0), axis=0, keepdims=True)


def one_hot(index_row, count):
    rows = lax.broadcasted_iota(jnp.int16, (count, index_row.shape[1]), 0)
    return jnp.where(rows == index_row.astype(jnp.int16), BF(1.0), BF(0.0))


def row_update(embedding, accum, gradient):
    accum = accum + jnp.mean(gradient * gradient, axis=1, keepdims=True)
    return embedding - learn_rate * gradient / jnp.sqrt(accum), accum


def count_batch(idx_ref, live, member, base, rows, first, half):
    source = idx_ref[member, pl.ds(base, 1), :] - first
    target = idx_ref[member, pl.ds(base + 1, 1), :]
    relation = idx_ref[member, pl.ds(base + 2, 1), :]
    negative = idx_ref[member, pl.ds(base + 3, 1), :]
    pair = jnp.where((source >= 0) & (source < half) & live, relation * half + source, -1)
    edges = dot(one_hot(target, rows), one_hot(pair, NREL * half), (1, 1))
    counts = dot(one_hot(negative, rows), jnp.ones((negative.shape[1], LANES), BF), (1, 0))
    return edges, jnp.stack([counts, jnp.where(counts > 0.0, 0.0, -3.0e38)])


def live_slots(idx_ref, bucket, nbatch):
    row = 8 * nbatch + bucket
    ends = [jnp.max(idx_ref[member, row : row + 1, :]) for member in range(idx_ref.shape[0])]
    for member in range(1, len(ends)):
        ends[member] = ends[member] + ends[member - 1]
    slots = []
    for slot in range(SLOTS):
        member, begin = jnp.int32(0), jnp.int32(0)
        for end in ends[:-1]:
            member = member + jnp.where(slot >= end, 1, 0)
            begin = jnp.where(slot >= end, end, begin)
        slots.append((slot < ends[-1], member, (bucket * nbatch + jnp.minimum(slot - begin, nbatch - 1)) * 4))
    return slots


def score_grads(scores_t, edges_ref, counts_ref, grad_bf):
    for start in range(0, scores_t.shape[1], LANES):
        cols = slice(start, start + LANES)
        score = scores_t[:, cols]
        total = 0.0
        for slot in range(SLOTS):
            counts = counts_ref[slot, 0]
            top = jnp.max(score + counts_ref[slot, 1], axis=0, keepdims=True)
            above = jnp.exp(jnp.minimum(score - top, 88.0))
            weighted = counts * above
            neg_total = jnp.sum(weighted, axis=0, keepdims=True)
            factor = edges_ref[slot, :, cols] / (above + neg_total)
            factor_sum = jnp.sum(factor, axis=0, keepdims=True)
            total += weighted * factor_sum - neg_total * factor
        grad_bf[:, cols] = total.astype(BF)


def queries_and_scores(left_bf, right_bf, op_ref, query_t, scores_t):
    half = left_bf.shape[0]
    for r in range(NREL):
        cols = slice(r * half, (r + 1) * half)
        query_t[:, cols] = dot(op_ref[r].astype(BF), left_bf, (1, 1)).astype(BF)
    scores_t[...] = dot(right_bf, query_t[...], (1, 0))


def table_products(table_t, op_ref):
    half = table_t.shape[1] // NREL
    return sum(dot(table_t[:, r * half : (r + 1) * half], op_ref[r].astype(BF), (0, 0)) for r in range(NREL))


def operator_products(table_t, left_bf, r):
    half = left_bf.shape[0]
    return dot(table_t[:, r * half : (r + 1) * half], left_bf, (1, 0))


def pack_rows(out_ref, embedding, accum):
    half, width = embedding.shape
    out_ref[0:half, :] = embedding
    row = jnp.concatenate([to_row(accum)] * (width // half), axis=1)
    out_ref[half : half + 8, :] = jnp.broadcast_to(row, (8, width))


def gather_kernel(nbatch, *refs):
    sources, staged, out_ref = refs[:5], refs[5:10], refs[10]
    held, buffers, sems = refs[11:16], refs[16:21], refs[21]
    pairs = [*zip(sources, buffers), *zip(staged, held)]
    copies = [pltpu.make_async_copy(*pair, sems.at[i]) for i, pair in enumerate(pairs)]
    for copy in copies:
        copy.start()
    out_ref[8 * nbatch :, :] = jnp.zeros_like(out_ref[8 * nbatch :, :])
    for copy in copies[: len(sources)]:
        copy.wait()
    *buffers, live_ref = buffers
    for bucket in range(2):
        row = 8 * nbatch + bucket
        out_ref[row : row + 1, :] = jnp.full((1, out_ref.shape[1]), live_ref[0, 0, bucket])
    for bucket in range(2):
        for batch in range(nbatch):
            for i, buffer in enumerate(buffers):
                row = (bucket * nbatch + batch) * 4 + i
                out_ref[row : row + 1, :] = buffer[0, 0, bucket, batch : batch + 1, :]
    for copy in copies[len(sources) :]:
        copy.wait()


def first_kernel(
    nbatch, idx_ref, left_all_ref, accum_ref, right_ref, op_ref, left_out, query_t, grad_bf, table_t,
    scores_t, edges_ref, counts_ref
):
    rows, width = right_ref.shape
    half = rows // 2
    first = pl.multiple_of(lax.axis_index("core") * half, half)
    left = left_all_ref[pl.ds(first, half), :]
    slots = live_slots(idx_ref, 0, nbatch)
    for slot, batch in enumerate(slots):
        edges_ref[slot], counts_ref[slot] = count_batch(idx_ref, *batch, rows, first, half)
    right_bf = right_ref[...].astype(BF)
    queries_and_scores(left.astype(BF), right_bf, op_ref, query_t, scores_t)
    score_grads(scores_t, edges_ref, counts_ref, grad_bf)
    table_t[...] = dot(right_bf, grad_bf[...], (0, 0)).astype(BF)
    left_grad = table_products(table_t, op_ref)
    accum = to_column(accum_ref[:, pl.ds(first, half)])
    pack_rows(left_out, *row_update(left, accum, left_grad))


def between_kernel(
    nbatch, idx_ref, left_ref, right_ref, accum_ref, op_ref, query_t, grad_bf, table_t,
    right_out, accum_out, grad_out, edges_out, counts_out,
    other_query_t, scores_t, other_grad_bf, edges_ref, counts_ref
):
    rows, width = right_ref.shape
    half = query_t.shape[1] // NREL
    core = lax.axis_index("core")
    mine = pl.multiple_of(core * half, half)
    other = pl.multiple_of((1 - core) * half, half)
    slots = live_slots(idx_ref, 0, nbatch)
    for slot, batch in enumerate(slots):
        edges_ref[slot], counts_ref[slot] = count_batch(idx_ref, *batch, rows, other, half)
    right = right_ref[...]
    right_bf = right.astype(BF)
    left_bf = left_ref[pl.ds(other, half), :].astype(BF)
    queries_and_scores(left_bf, right_bf, op_ref, other_query_t, scores_t)
    slots = live_slots(idx_ref, 1, nbatch)
    for slot, batch in enumerate(slots):
        edges_out[slot], counts_out[slot] = count_batch(idx_ref, *batch, rows, 0, rows)
    score_grads(scores_t, edges_ref, counts_ref, other_grad_bf)
    right_grad = dot(grad_bf[...], query_t[...], (1, 1)) + dot(other_grad_bf[...], other_query_t[...], (1, 1))
    right_out[...], accum = row_update(right, to_column(accum_ref[...]), right_grad)
    accum_out[...] = to_row(accum)
    cols = pl.ds(mine, half)
    other_table_t = dot(right_bf, other_grad_bf[:, cols], (0, 0)).astype(BF)
    my_left_bf = left_ref[pl.ds(mine, half), :].astype(BF)
    grad_out[...] = dot(table_t[:, cols], my_left_bf, (1, 0)) + dot(other_table_t, left_bf, (1, 0))


def second_kernel(
    edges_ref, counts_ref, left_ref, right_ref, accum_ref, op_ref, grad_ref,
    left_out, left_accum_out, right_out, right_accum_out, grad_out, query_t, scores_t, grad_bf, table_t
):
    nrel = op_ref.shape[0]
    rows, width = right_ref.shape
    half = rows // 2
    left = jnp.concatenate([left_ref[0, 0:half, :], left_ref[1, 0:half, :]], axis=0)
    left_accum = jnp.concatenate([left_ref[0, half : half + 1, 0:half], left_ref[1, half : half + 1, 0:half]], axis=1)
    right = right_ref[...]
    left_bf, right_bf = left.astype(BF), right.astype(BF)
    queries_and_scores(left_bf, right_bf, op_ref, query_t, scores_t)
    score_grads(scores_t, edges_ref, counts_ref, grad_bf)
    table_t[...] = dot(right_bf, grad_bf[...], (0, 0)).astype(BF)
    mine = pl.ds(pl.multiple_of(lax.axis_index("core") * rows, rows), rows)
    grad = dot(table_t[:, mine], left_bf, (1, 0)) + grad_ref[...]
    for part in range(2):
        grad_out[part] = grad[:, part * 128 : (part + 1) * 128].reshape(grad_out.shape[1:])
    left_grad = jnp.zeros((rows, width), F32)
    for r in range(nrel):
        left_grad += dot(table_t[:, r * rows : (r + 1) * rows], op_ref[r].astype(BF), (0, 0))
    left_out[...], accum = row_update(left, to_column(left_accum), left_grad)
    left_accum_out[...] = to_row(accum)
    right_grad = dot(grad_bf[...], query_t[...], (1, 1))
    right_out[...], accum = row_update(right, to_column(accum_ref[...]), right_grad)
    right_accum_out[...] = to_row(accum)


def final_kernel(total_ref, relation_ref, state_ref, *refs):
    rows_refs, rows_hbm = refs[:4], refs[6:10]
    relation_hbm, state_hbm, relation_out, state_out, sems = *refs[4:6], *refs[10:13]
    nrel, width, _ = relation_ref.shape
    copies = [pltpu.make_async_copy(here, there, sems.at[i]) for i, (here, there) in enumerate(zip(rows_refs, rows_hbm))]
    for copy in copies:
        copy.start()
    for r in range(nrel):
        for part in range(2):
            cols = slice(part * 128, (part + 1) * 128)
            grad = total_ref[r, part].reshape(width, 128)
            state = state_ref[r, :, cols] + grad * grad
            state_out[r, :, cols] = state
            relation_out[r, :, cols] = relation_ref[r, :, cols] - learn_rate * grad / jnp.sqrt(state)
        for here, there in ((relation_out, relation_hbm), (state_out, state_hbm)):
            copies.append(pltpu.make_async_copy(here.at[r], there.at[r], sems.at[len(copies)]))
            copies[-1].start()
    for copy in copies:
        copy.wait()


def f32(*shape):
    return jax.ShapeDtypeStruct(shape, F32)


def call(kernel, name, outs, args, scratch=(), flops=0, outside=(), outputs_outside=False):
    out_space = pltpu.HBM if outputs_outside else pltpu.VMEM
    spaces = [pltpu.HBM if i in outside else pltpu.VMEM for i in range(len(args))]
    sems = [pltpu.SemaphoreType.DMA((len(outside),))] if outside else []
    return pl.pallas_call(
        kernel,
        out_shape=outs,
        in_specs=[pl.BlockSpec(memory_space=space) for space in spaces],
        out_specs=[pl.BlockSpec(memory_space=out_space)] * len(outs),
        scratch_shapes=[pltpu.VMEM(*one) if isinstance(one, tuple) else one for one in scratch] + sems,
        compiler_params=pltpu.CompilerParams(vmem_limit_bytes=30 << 20),
        cost_estimate=pl.CostEstimate(flops=flops, bytes_accessed=4 << 20, transcendentals=0),
        name=name,
    )(*(pltpu.with_memory_space_constraint(a, pltpu.HBM) if i in outside else a for i, a in enumerate(args)))


def buckets(index, left, left_accum, right, right_accum, relation, nbatch, move):
    nrel, width, _ = relation.shape
    rows = left.shape[0]
    pairs = nrel * rows
    half = rows // 2
    mine = NREL * half
    bf16 = lambda *shape: jax.ShapeDtypeStruct(shape, BF)
    counts = [((SLOTS, rows, mine), F32), ((SLOTS, 2, rows, LANES), F32)]
    moved, query_t, grad_bf, table_t = call(
        functools.partial(first_kernel, nbatch),
        "bucket0_left",
        (f32(half + 8, width), bf16(width, mine), bf16(rows, mine), bf16(width, mine)),
        (index, left, left_accum, right, relation),
        [((rows, mine), F32), *counts],
        flops=2 << 30,
    )
    moved = move(moved)
    right, right_accum, grad, edges, counts = call(
        functools.partial(between_kernel, nbatch),
        "bucket0_right",
        (f32(rows, width), f32(1, rows), f32(width, width), f32(SLOTS, rows, pairs), f32(SLOTS, 2, rows, LANES)),
        (index, left, right, right_accum, relation, query_t, grad_bf, table_t),
        [((width, mine), BF), ((rows, mine), F32), ((rows, mine), BF), *counts],
        flops=1 << 30,
    )
    moved = lax.all_gather(moved, "core", axis=0, tiled=False)
    return call(
        second_kernel,
        "bucket1",
        (f32(rows, width), f32(1, rows), f32(rows, width), f32(1, rows), f32(2, width // 4, 4, 128)),
        (edges, counts, moved, right, right_accum, relation, grad),
        [((width, pairs), BF), ((rows, pairs), F32), ((rows, pairs), BF), ((width, pairs), BF)],
        flops=2 << 30,
    )


def body(
    left_emb,
    left_state,
    right_emb,
    right_state,
    relation,
    relation_state,
    edge_src,
    edge_dst,
    edge_rel,
    negatives,
    batch_counts,
):
    nbatch, batch = edge_src.shape[3:]
    rows, width = left_emb.shape
    blocks = lax.axis_size(BLK)
    index_rows = -(-(8 * nbatch + 2) // 8) * 8
    arrays = (left_emb, left_state.reshape(1, rows), right_emb, right_state.reshape(1, rows), relation)
    index, *arrays = call(
        functools.partial(gather_kernel, nbatch),
        "gather_index",
        (jax.ShapeDtypeStruct((index_rows, batch), jnp.int32), *(f32(*array.shape) for array in arrays)),
        (edge_src, edge_dst, edge_rel, negatives, batch_counts, *arrays),
        [(edge_src.shape, jnp.int32)] * 4 + [pltpu.SMEM(batch_counts.shape, jnp.int32)],
        outside=tuple(range(10)),
    )
    index = lax.all_gather(index, REP, axis=0, tiled=False)
    route = [(i, (i + 1) % blocks) for i in range(blocks)]
    left, left_accum, right, right_accum, grad = buckets(
        index,
        *arrays,
        nbatch,
        lambda half: lax.ppermute(half, BLK, route),
    )
    grad = grad.reshape(blocks, -1, 128)
    grad = jnp.sum(lax.all_to_all(grad, BLK, 0, 0, tiled=True), axis=0)
    grad = jnp.broadcast_to(grad[None], (blocks, *grad.shape))
    grad = lax.all_to_all(grad, BLK, 0, 0, tiled=True)
    grad = lax.all_gather(grad, "core", axis=0, tiled=False)
    grad = grad.reshape(relation.shape[0], 2, width // 4, 4, 128)
    updated = (left, left_accum, right, right_accum)
    relation_new, relation_state_new, left, left_accum, right, right_accum = call(
        final_kernel,
        "final_update",
        tuple(f32(*array.shape) for array in (relation, relation_state, *updated)),
        (grad, arrays[-1], relation_state, *updated),
        [(relation.shape, F32)] * 2 + [pltpu.SemaphoreType.DMA((8,))],
        outputs_outside=True,
    )
    return (
        left,
        left_accum.reshape(rows),
        right,
        right_accum.reshape(rows),
        relation_new,
        relation_state_new,
    )


def solution(mesh):
    sizes = (8, 8, 2, 2, 2)
    mesh = jax.sharding.Mesh(mesh.devices.reshape(sizes), (*BLK, *REP))
    row, edge = P(BLK, None), P(BLK, REP, None, None, None)
    in_specs = (row, P(BLK), row, P(BLK), P(), P(), edge, edge, edge, edge, P(BLK, REP, None))
    out_specs = (row, P(BLK), row, P(BLK), P(), P())
    return jax.shard_map(body, mesh=mesh, in_specs=in_specs, out_specs=out_specs, check_vma=False)
```

```python
import functools

import jax
import jax.numpy as jnp
from jax import lax
from jax.experimental import pallas as pl
from jax.experimental.pallas import tpu as pltpu
from jax.sharding import PartitionSpec as P

learn_rate = 0.1
BF = jnp.bfloat16
F32 = jnp.float32
BLK = ("z", "y", "xl")
REP = ("xh", "core")
NREL = 2
LANES = 128
SLOTS = 4


def dot(a, b, dims):
    return lax.dot_general(a, b, ((dims[:1], dims[1:]), ((), ())), preferred_element_type=F32)


def same(size):
    shape = (size, size)
    return lax.broadcasted_iota(jnp.int32, shape, 0) == lax.broadcasted_iota(jnp.int32, shape, 1)


def to_column(row):
    return jnp.sum(jnp.where(same(row.shape[1]), row, 0.0), axis=1, keepdims=True)


def to_row(column):
    return jnp.sum(jnp.where(same(column.shape[0]), column, 0.0), axis=0, keepdims=True)


def one_hot(index_row, count):
    rows = lax.broadcasted_iota(jnp.int16, (count, index_row.shape[1]), 0)
    return jnp.where(rows == index_row.astype(jnp.int16), BF(1.0), BF(0.0))


def row_update(embedding, accum, gradient):
    accum = accum + jnp.mean(gradient * gradient, axis=1, keepdims=True)
    return embedding - learn_rate * gradient / jnp.sqrt(accum), accum


def count_batch(idx_ref, live, member, base, rows, first, half):
    source = idx_ref[member, pl.ds(base, 1), :] - first
    target = idx_ref[member, pl.ds(base + 1, 1), :]
    relation = idx_ref[member, pl.ds(base + 2, 1), :]
    negative = idx_ref[member, pl.ds(base + 3, 1), :]
    pair = jnp.where((source >= 0) & (source < half) & live, relation * half + source, -1)
    edges = dot(one_hot(target, rows), one_hot(pair, NREL * half), (1, 1))
    counts = dot(one_hot(negative, rows), jnp.ones((negative.shape[1], LANES), BF), (1, 0))
    return edges, jnp.stack([counts, jnp.where(counts > 0.0, 0.0, -3.0e38)])


def live_slots(idx_ref, bucket, nbatch):
    row = 8 * nbatch + bucket
    ends = [jnp.max(idx_ref[member, row : row + 1, :]) for member in range(idx_ref.shape[0])]
    for member in range(1, len(ends)):
        ends[member] = ends[member] + ends[member - 1]
    slots = []
    for slot in range(SLOTS):
        member, begin = jnp.int32(0), jnp.int32(0)
        for end in ends[:-1]:
            member = member + jnp.where(slot >= end, 1, 0)
            begin = jnp.where(slot >= end, end, begin)
        slots.append((slot < ends[-1], member, (bucket * nbatch + jnp.minimum(slot - begin, nbatch - 1)) * 4))
    return slots


def score_grads(scores_t, edges_ref, counts_ref, grad_bf, rest_bf=None):
    for start in range(0, scores_t.shape[1], LANES):
        cols = slice(start, start + LANES)
        score = scores_t[:, cols]
        total = 0.0
        for slot in range(SLOTS):
            counts = counts_ref[slot, 0]
            top = jnp.max(score + counts_ref[slot, 1], axis=0, keepdims=True)
            above = jnp.exp(jnp.minimum(score - top, 88.0))
            weighted = counts * above
            neg_total = jnp.sum(weighted, axis=0, keepdims=True)
            factor = edges_ref[slot, :, cols] / (above + neg_total)
            factor_sum = jnp.sum(factor, axis=0, keepdims=True)
            total += weighted * factor_sum - neg_total * factor
        rounded = total.astype(BF)
        grad_bf[:, cols] = rounded
        if rest_bf is not None:
            rest_bf[:, cols] = (total - rounded.astype(F32)).astype(BF)


def queries_and_scores(left_bf, right_bf, op_ref, query_t, scores_t):
    half = left_bf.shape[0]
    for r in range(NREL):
        cols = slice(r * half, (r + 1) * half)
        query_t[:, cols] = dot(op_ref[r].astype(BF), left_bf, (1, 1)).astype(BF)
    scores_t[...] = dot(right_bf, query_t[...], (1, 0))


def table_products(table_t, op_ref):
    half = table_t.shape[1] // NREL
    return sum(dot(table_t[:, r * half : (r + 1) * half], op_ref[r].astype(BF), (0, 0)) for r in range(NREL))


def operator_products(table_t, left_bf, r):
    half = left_bf.shape[0]
    return dot(table_t[:, r * half : (r + 1) * half], left_bf, (1, 0))


def pack_rows(out_ref, embedding, accum):
    half, width = embedding.shape
    out_ref[0:half, :] = embedding
    row = jnp.concatenate([to_row(accum)] * (width // half), axis=1)
    out_ref[half : half + 8, :] = jnp.broadcast_to(row, (8, width))


def gather_kernel(nbatch, *refs):
    sources, staged, out_ref = refs[:5], refs[5:10], refs[10]
    held, buffers, sems = refs[11:16], refs[16:21], refs[21]
    pairs = [*zip(sources, buffers), *zip(staged, held)]
    copies = [pltpu.make_async_copy(*pair, sems.at[i]) for i, pair in enumerate(pairs)]
    for copy in copies:
        copy.start()
    out_ref[8 * nbatch :, :] = jnp.zeros_like(out_ref[8 * nbatch :, :])
    for copy in copies[: len(sources)]:
        copy.wait()
    *buffers, live_ref = buffers
    for bucket in range(2):
        row = 8 * nbatch + bucket
        out_ref[row : row + 1, :] = jnp.full((1, out_ref.shape[1]), live_ref[0, 0, bucket])
    for bucket in range(2):
        for batch in range(nbatch):
            for i, buffer in enumerate(buffers):
                row = (bucket * nbatch + batch) * 4 + i
                out_ref[row : row + 1, :] = buffer[0, 0, bucket, batch : batch + 1, :]
    for copy in copies[len(sources) :]:
        copy.wait()


def first_kernel(
    nbatch, idx_ref, left_all_ref, accum_ref, right_ref, op_ref, left_out, query_t, grad_bf, rest_bf, table_t,
    scores_t, edges_ref, counts_ref
):
    rows, width = right_ref.shape
    half = rows // 2
    first = pl.multiple_of(lax.axis_index("core") * half, half)
    left = left_all_ref[pl.ds(first, half), :]
    slots = live_slots(idx_ref, 0, nbatch)
    for slot, batch in enumerate(slots):
        edges_ref[slot], counts_ref[slot] = count_batch(idx_ref, *batch, rows, first, half)
    right_bf = right_ref[...].astype(BF)
    queries_and_scores(left.astype(BF), right_bf, op_ref, query_t, scores_t)
    score_grads(scores_t, edges_ref, counts_ref, grad_bf, rest_bf)
    table = dot(right_bf, grad_bf[...], (0, 0)) + dot(right_bf, rest_bf[...], (0, 0))
    table_t[...] = table.astype(BF)
    left_grad = table_products(table_t, op_ref)
    accum = to_column(accum_ref[:, pl.ds(first, half)])
    pack_rows(left_out, *row_update(left, accum, left_grad))


def between_kernel(
    nbatch, idx_ref, left_ref, right_ref, accum_ref, op_ref, query_t, grad_bf, rest_bf, table_t,
    right_out, accum_out, grad_out, edges_out, counts_out,
    other_query_t, scores_t, other_grad_bf, other_rest_bf, edges_ref, counts_ref
):
    rows, width = right_ref.shape
    half = query_t.shape[1] // NREL
    core = lax.axis_index("core")
    mine = pl.multiple_of(core * half, half)
    other = pl.multiple_of((1 - core) * half, half)
    slots = live_slots(idx_ref, 0, nbatch)
    for slot, batch in enumerate(slots):
        edges_ref[slot], counts_ref[slot] = count_batch(idx_ref, *batch, rows, other, half)
    right = right_ref[...]
    right_bf = right.astype(BF)
    left_bf = left_ref[pl.ds(other, half), :].astype(BF)
    queries_and_scores(left_bf, right_bf, op_ref, other_query_t, scores_t)
    slots = live_slots(idx_ref, 1, nbatch)
    for slot, batch in enumerate(slots):
        edges_out[slot], counts_out[slot] = count_batch(idx_ref, *batch, rows, 0, rows)
    score_grads(scores_t, edges_ref, counts_ref, other_grad_bf, other_rest_bf)
    my_grad = dot(grad_bf[...], query_t[...], (1, 1)) + dot(rest_bf[...], query_t[...], (1, 1))
    other_grad = dot(other_grad_bf[...], other_query_t[...], (1, 1)) + dot(other_rest_bf[...], other_query_t[...], (1, 1))
    right_grad = my_grad + other_grad
    right_out[...], accum = row_update(right, to_column(accum_ref[...]), right_grad)
    accum_out[...] = to_row(accum)
    cols = pl.ds(mine, half)
    other_table = dot(right_bf, other_grad_bf[:, cols], (0, 0)) + dot(right_bf, other_rest_bf[:, cols], (0, 0))
    other_table_t = other_table.astype(BF)
    my_left_bf = left_ref[pl.ds(mine, half), :].astype(BF)
    grad_out[...] = dot(table_t[:, cols], my_left_bf, (1, 0)) + dot(other_table_t, left_bf, (1, 0))


def second_kernel(
    edges_ref, counts_ref, left_ref, right_ref, accum_ref, op_ref, grad_ref,
    left_out, left_accum_out, right_out, right_accum_out, grad_out, query_t, scores_t, grad_bf, table_t
):
    nrel = op_ref.shape[0]
    rows, width = right_ref.shape
    half = rows // 2
    left = jnp.concatenate([left_ref[0, 0:half, :], left_ref[1, 0:half, :]], axis=0)
    left_accum = jnp.concatenate([left_ref[0, half : half + 1, 0:half], left_ref[1, half : half + 1, 0:half]], axis=1)
    right = right_ref[...]
    left_bf, right_bf = left.astype(BF), right.astype(BF)
    queries_and_scores(left_bf, right_bf, op_ref, query_t, scores_t)
    score_grads(scores_t, edges_ref, counts_ref, grad_bf)
    table_t[...] = dot(right_bf, grad_bf[...], (0, 0)).astype(BF)
    mine = pl.ds(pl.multiple_of(lax.axis_index("core") * rows, rows), rows)
    grad = dot(table_t[:, mine], left_bf, (1, 0)) + grad_ref[...]
    for part in range(2):
        grad_out[part] = grad[:, part * 128 : (part + 1) * 128].reshape(grad_out.shape[1:])
    left_grad = jnp.zeros((rows, width), F32)
    for r in range(nrel):
        left_grad += dot(table_t[:, r * rows : (r + 1) * rows], op_ref[r].astype(BF), (0, 0))
    left_out[...], accum = row_update(left, to_column(left_accum), left_grad)
    left_accum_out[...] = to_row(accum)
    right_grad = dot(grad_bf[...], query_t[...], (1, 1))
    right_out[...], accum = row_update(right, to_column(accum_ref[...]), right_grad)
    right_accum_out[...] = to_row(accum)


def final_kernel(total_ref, relation_ref, state_ref, *refs):
    rows_refs, rows_hbm = refs[:4], refs[6:10]
    relation_hbm, state_hbm, relation_out, state_out, sems = *refs[4:6], *refs[10:13]
    nrel, width, _ = relation_ref.shape
    copies = [pltpu.make_async_copy(here, there, sems.at[i]) for i, (here, there) in enumerate(zip(rows_refs, rows_hbm))]
    for copy in copies:
        copy.start()
    for r in range(nrel):
        for part in range(2):
            cols = slice(part * 128, (part + 1) * 128)
            grad = total_ref[r, part].reshape(width, 128)
            state = state_ref[r, :, cols] + grad * grad
            state_out[r, :, cols] = state
            relation_out[r, :, cols] = relation_ref[r, :, cols] - learn_rate * grad / jnp.sqrt(state)
        for here, there in ((relation_out, relation_hbm), (state_out, state_hbm)):
            copies.append(pltpu.make_async_copy(here.at[r], there.at[r], sems.at[len(copies)]))
            copies[-1].start()
    for copy in copies:
        copy.wait()


def f32(*shape):
    return jax.ShapeDtypeStruct(shape, F32)


def call(kernel, name, outs, args, scratch=(), flops=0, outside=(), outputs_outside=False):
    out_space = pltpu.HBM if outputs_outside else pltpu.VMEM
    spaces = [pltpu.HBM if i in outside else pltpu.VMEM for i in range(len(args))]
    sems = [pltpu.SemaphoreType.DMA((len(outside),))] if outside else []
    return pl.pallas_call(
        kernel,
        out_shape=outs,
        in_specs=[pl.BlockSpec(memory_space=space) for space in spaces],
        out_specs=[pl.BlockSpec(memory_space=out_space)] * len(outs),
        scratch_shapes=[pltpu.VMEM(*one) if isinstance(one, tuple) else one for one in scratch] + sems,
        compiler_params=pltpu.CompilerParams(vmem_limit_bytes=30 << 20),
        cost_estimate=pl.CostEstimate(flops=flops, bytes_accessed=4 << 20, transcendentals=0),
        name=name,
    )(*(pltpu.with_memory_space_constraint(a, pltpu.HBM) if i in outside else a for i, a in enumerate(args)))


def buckets(index, left, left_accum, right, right_accum, relation, nbatch, move):
    nrel, width, _ = relation.shape
    rows = left.shape[0]
    pairs = nrel * rows
    half = rows // 2
    mine = NREL * half
    bf16 = lambda *shape: jax.ShapeDtypeStruct(shape, BF)
    counts = [((SLOTS, rows, mine), F32), ((SLOTS, 2, rows, LANES), F32)]
    moved, query_t, grad_bf, rest_bf, table_t = call(
        functools.partial(first_kernel, nbatch),
        "bucket0_left",
        (f32(half + 8, width), bf16(width, mine), bf16(rows, mine), bf16(rows, mine), bf16(width, mine)),
        (index, left, left_accum, right, relation),
        [((rows, mine), F32), *counts],
        flops=2 << 30,
    )
    moved = move(moved)
    right, right_accum, grad, edges, counts = call(
        functools.partial(between_kernel, nbatch),
        "bucket0_right",
        (f32(rows, width), f32(1, rows), f32(width, width), f32(SLOTS, rows, pairs), f32(SLOTS, 2, rows, LANES)),
        (index, left, right, right_accum, relation, query_t, grad_bf, rest_bf, table_t),
        [((width, mine), BF), ((rows, mine), F32), ((rows, mine), BF), ((rows, mine), BF), *counts],
        flops=1 << 30,
    )
    moved = lax.all_gather(moved, "core", axis=0, tiled=False)
    return call(
        second_kernel,
        "bucket1",
        (f32(rows, width), f32(1, rows), f32(rows, width), f32(1, rows), f32(2, width // 4, 4, 128)),
        (edges, counts, moved, right, right_accum, relation, grad),
        [((width, pairs), BF), ((rows, pairs), F32), ((rows, pairs), BF), ((width, pairs), BF)],
        flops=2 << 30,
    )


def body(
    left_emb,
    left_state,
    right_emb,
    right_state,
    relation,
    relation_state,
    edge_src,
    edge_dst,
    edge_rel,
    negatives,
    batch_counts,
):
    nbatch, batch = edge_src.shape[3:]
    rows, width = left_emb.shape
    blocks = lax.axis_size(BLK)
    index_rows = -(-(8 * nbatch + 2) // 8) * 8
    arrays = (left_emb, left_state.reshape(1, rows), right_emb, right_state.reshape(1, rows), relation)
    index, *arrays = call(
        functools.partial(gather_kernel, nbatch),
        "gather_index",
        (jax.ShapeDtypeStruct((index_rows, batch), jnp.int32), *(f32(*array.shape) for array in arrays)),
        (edge_src, edge_dst, edge_rel, negatives, batch_counts, *arrays),
        [(edge_src.shape, jnp.int32)] * 4 + [pltpu.SMEM(batch_counts.shape, jnp.int32)],
        outside=tuple(range(10)),
    )
    index = lax.all_gather(index, REP, axis=0, tiled=False)
    route = [(i, (i + 1) % blocks) for i in range(blocks)]
    left, left_accum, right, right_accum, grad = buckets(
        index,
        *arrays,
        nbatch,
        lambda half: lax.ppermute(half, BLK, route),
    )
    grad = grad.reshape(blocks, -1, 128)
    grad = jnp.sum(lax.all_to_all(grad, BLK, 0, 0, tiled=True), axis=0)
    grad = jnp.broadcast_to(grad[None], (blocks, *grad.shape))
    grad = lax.all_to_all(grad, BLK, 0, 0, tiled=True)
    grad = lax.all_gather(grad, "core", axis=0, tiled=False)
    grad = grad.reshape(relation.shape[0], 2, width // 4, 4, 128)
    updated = (left, left_accum, right, right_accum)
    relation_new, relation_state_new, left, left_accum, right, right_accum = call(
        final_kernel,
        "final_update",
        tuple(f32(*array.shape) for array in (relation, relation_state, *updated)),
        (grad, arrays[-1], relation_state, *updated),
        [(relation.shape, F32)] * 2 + [pltpu.SemaphoreType.DMA((8,))],
        outputs_outside=True,
    )
    return (
        left,
        left_accum.reshape(rows),
        right,
        right_accum.reshape(rows),
        relation_new,
        relation_state_new,
    )


def solution(mesh):
    sizes = (8, 8, 2, 2, 2)
    mesh = jax.sharding.Mesh(mesh.devices.reshape(sizes), (*BLK, *REP))
    row, edge = P(BLK, None), P(BLK, REP, None, None, None)
    in_specs = (row, P(BLK), row, P(BLK), P(), P(), edge, edge, edge, edge, P(BLK, REP, None))
    out_specs = (row, P(BLK), row, P(BLK), P(), P())
    return jax.shard_map(body, mesh=mesh, in_specs=in_specs, out_specs=out_specs, check_vma=False)
```

```python
import functools

import jax
import jax.numpy as jnp
from jax import lax
from jax.experimental import pallas as pl
from jax.experimental.pallas import tpu as pltpu
from jax.sharding import PartitionSpec as P

learn_rate = 0.1
BF = jnp.bfloat16
F32 = jnp.float32
BLK = ("z", "y", "xl")
REP = ("xh", "core")
NREL = 2
LANES = 256
SLOTS = 4


def dot(a, b, dims):
    return lax.dot_general(a, b, ((dims[:1], dims[1:]), ((), ())), preferred_element_type=F32)


def same(size):
    shape = (size, size)
    return lax.broadcasted_iota(jnp.int32, shape, 0) == lax.broadcasted_iota(jnp.int32, shape, 1)


def to_column(row):
    return jnp.sum(jnp.where(same(row.shape[1]), row, 0.0), axis=1, keepdims=True)


def to_row(column):
    return jnp.sum(jnp.where(same(column.shape[0]), column, 0.0), axis=0, keepdims=True)


def one_hot(index_row, count):
    rows = lax.broadcasted_iota(jnp.int16, (count, index_row.shape[1]), 0)
    return jnp.where(rows == index_row.astype(jnp.int16), BF(1.0), BF(0.0))


def row_update(embedding, accum, gradient):
    accum = accum + jnp.mean(gradient * gradient, axis=1, keepdims=True)
    return embedding - learn_rate * gradient / jnp.sqrt(accum), accum


def count_batch(idx_ref, live, member, base, rows, first, half):
    source = idx_ref[member, pl.ds(base, 1), :] - first
    target = idx_ref[member, pl.ds(base + 1, 1), :]
    relation = idx_ref[member, pl.ds(base + 2, 1), :]
    negative = idx_ref[member, pl.ds(base + 3, 1), :]
    pair = jnp.where((source >= 0) & (source < half) & live, relation * half + source, -1)
    edges = dot(one_hot(target, rows), one_hot(pair, NREL * half), (1, 1))
    counts = dot(one_hot(negative, rows), jnp.ones((negative.shape[1], LANES), BF), (1, 0))
    return edges, jnp.stack([counts, jnp.where(counts > 0.0, 0.0, -3.0e38)])


def live_slots(idx_ref, bucket, nbatch):
    row = 8 * nbatch + bucket
    ends = [jnp.max(idx_ref[member, row : row + 1, :]) for member in range(idx_ref.shape[0])]
    for member in range(1, len(ends)):
        ends[member] = ends[member] + ends[member - 1]
    slots = []
    for slot in range(SLOTS):
        member, begin = jnp.int32(0), jnp.int32(0)
        for end in ends[:-1]:
            member = member + jnp.where(slot >= end, 1, 0)
            begin = jnp.where(slot >= end, end, begin)
        slots.append((slot < ends[-1], member, (bucket * nbatch + jnp.minimum(slot - begin, nbatch - 1)) * 4))
    return slots


def score_grads(scores_t, edges_ref, counts_ref, grad_bf):
    for start in range(0, scores_t.shape[1], LANES):
        cols = slice(start, start + LANES)
        score = scores_t[:, cols]
        total = 0.0
        for slot in range(SLOTS):
            counts = counts_ref[slot, 0]
            top = jnp.max(score + counts_ref[slot, 1], axis=0, keepdims=True)
            above = jnp.exp(jnp.minimum(score - top, 88.0))
            weighted = counts * above
            neg_total = jnp.sum(weighted, axis=0, keepdims=True)
            factor = edges_ref[slot, :, cols] / (above + neg_total)
            factor_sum = jnp.sum(factor, axis=0, keepdims=True)
            total += weighted * factor_sum - neg_total * factor
        grad_bf[:, cols] = total.astype(BF)


def queries_and_scores(left_bf, right_bf, op_ref, query_t, scores_t):
    half = left_bf.shape[0]
    for r in range(NREL):
        cols = slice(r * half, (r + 1) * half)
        query_t[:, cols] = dot(op_ref[r].astype(BF), left_bf, (1, 1)).astype(BF)
    scores_t[...] = dot(right_bf, query_t[...], (1, 0))


def table_products(table_t, op_ref):
    half = table_t.shape[1] // NREL
    return sum(dot(table_t[:, r * half : (r + 1) * half], op_ref[r].astype(BF), (0, 0)) for r in range(NREL))


def operator_products(table_t, left_bf, r):
    half = left_bf.shape[0]
    return dot(table_t[:, r * half : (r + 1) * half], left_bf, (1, 0))


def pack_rows(out_ref, embedding, accum):
    half, width = embedding.shape
    out_ref[0:half, :] = embedding
    row = jnp.concatenate([to_row(accum)] * (width // half), axis=1)
    out_ref[half : half + 8, :] = jnp.broadcast_to(row, (8, width))


def gather_kernel(nbatch, *refs):
    sources, staged, out_ref = refs[:5], refs[5:10], refs[10]
    held, buffers, sems = refs[11:16], refs[16:21], refs[21]
    pairs = [*zip(sources, buffers), *zip(staged, held)]
    copies = [pltpu.make_async_copy(*pair, sems.at[i]) for i, pair in enumerate(pairs)]
    for copy in copies:
        copy.start()
    out_ref[8 * nbatch :, :] = jnp.zeros_like(out_ref[8 * nbatch :, :])
    for copy in copies[: len(sources)]:
        copy.wait()
    *buffers, live_ref = buffers
    for bucket in range(2):
        row = 8 * nbatch + bucket
        out_ref[row : row + 1, :] = jnp.full((1, out_ref.shape[1]), live_ref[0, 0, bucket])
    for bucket in range(2):
        for batch in range(nbatch):
            for i, buffer in enumerate(buffers):
                row = (bucket * nbatch + batch) * 4 + i
                out_ref[row : row + 1, :] = buffer[0, 0, bucket, batch : batch + 1, :]
    for copy in copies[len(sources) :]:
        copy.wait()


def first_kernel(
    nbatch, idx_ref, left_all_ref, accum_ref, right_ref, op_ref, left_out, query_t, grad_bf, table_t,
    scores_t, edges_ref, counts_ref
):
    rows, width = right_ref.shape
    half = rows // 2
    first = pl.multiple_of(lax.axis_index("core") * half, half)
    left = left_all_ref[pl.ds(first, half), :]
    slots = live_slots(idx_ref, 0, nbatch)
    for slot, batch in enumerate(slots):
        edges_ref[slot], counts_ref[slot] = count_batch(idx_ref, *batch, rows, first, half)
    right_bf = right_ref[...].astype(BF)
    queries_and_scores(left.astype(BF), right_bf, op_ref, query_t, scores_t)
    score_grads(scores_t, edges_ref, counts_ref, grad_bf)
    table_t[...] = dot(right_bf, grad_bf[...], (0, 0)).astype(BF)
    left_grad = table_products(table_t, op_ref)
    accum = to_column(accum_ref[:, pl.ds(first, half)])
    pack_rows(left_out, *row_update(left, accum, left_grad))


def between_kernel(
    nbatch, idx_ref, left_ref, right_ref, accum_ref, op_ref, query_t, grad_bf, table_t,
    right_out, accum_out, grad_out, edges_out, counts_out,
    other_query_t, scores_t, other_grad_bf, edges_ref, counts_ref
):
    rows, width = right_ref.shape
    half = query_t.shape[1] // NREL
    core = lax.axis_index("core")
    mine = pl.multiple_of(core * half, half)
    other = pl.multiple_of((1 - core) * half, half)
    slots = live_slots(idx_ref, 0, nbatch)
    for slot, batch in enumerate(slots):
        edges_ref[slot], counts_ref[slot] = count_batch(idx_ref, *batch, rows, other, half)
    right = right_ref[...]
    right_bf = right.astype(BF)
    left_bf = left_ref[pl.ds(other, half), :].astype(BF)
    queries_and_scores(left_bf, right_bf, op_ref, other_query_t, scores_t)
    slots = live_slots(idx_ref, 1, nbatch)
    for slot, batch in enumerate(slots):
        edges_out[slot], counts_out[slot] = count_batch(idx_ref, *batch, rows, 0, rows)
    score_grads(scores_t, edges_ref, counts_ref, other_grad_bf)
    right_grad = dot(grad_bf[...], query_t[...], (1, 1)) + dot(other_grad_bf[...], other_query_t[...], (1, 1))
    right_out[...], accum = row_update(right, to_column(accum_ref[...]), right_grad)
    accum_out[...] = to_row(accum)
    cols = pl.ds(mine, half)
    other_table_t = dot(right_bf, other_grad_bf[:, cols], (0, 0)).astype(BF)
    my_left_bf = left_ref[pl.ds(mine, half), :].astype(BF)
    grad_out[...] = dot(table_t[:, cols], my_left_bf, (1, 0)) + dot(other_table_t, left_bf, (1, 0))


def second_kernel(
    edges_ref, counts_ref, left_ref, right_ref, accum_ref, op_ref, grad_ref,
    left_out, left_accum_out, right_out, right_accum_out, grad_out, query_t, scores_t, grad_bf, table_t
):
    nrel = op_ref.shape[0]
    rows, width = right_ref.shape
    half = rows // 2
    left = jnp.concatenate([left_ref[0, 0:half, :], left_ref[1, 0:half, :]], axis=0)
    left_accum = jnp.concatenate([left_ref[0, half : half + 1, 0:half], left_ref[1, half : half + 1, 0:half]], axis=1)
    right = right_ref[...]
    left_bf, right_bf = left.astype(BF), right.astype(BF)
    queries_and_scores(left_bf, right_bf, op_ref, query_t, scores_t)
    score_grads(scores_t, edges_ref, counts_ref, grad_bf)
    table_t[...] = dot(right_bf, grad_bf[...], (0, 0)).astype(BF)
    mine = pl.ds(pl.multiple_of(lax.axis_index("core") * rows, rows), rows)
    grad = dot(table_t[:, mine], left_bf, (1, 0)) + grad_ref[...]
    for part in range(2):
        grad_out[part] = grad[:, part * 128 : (part + 1) * 128].reshape(grad_out.shape[1:])
    left_grad = jnp.zeros((rows, width), F32)
    for r in range(nrel):
        left_grad += dot(table_t[:, r * rows : (r + 1) * rows], op_ref[r].astype(BF), (0, 0))
    left_out[...], accum = row_update(left, to_column(left_accum), left_grad)
    left_accum_out[...] = to_row(accum)
    right_grad = dot(grad_bf[...], query_t[...], (1, 1))
    right_out[...], accum = row_update(right, to_column(accum_ref[...]), right_grad)
    right_accum_out[...] = to_row(accum)


def final_kernel(total_ref, relation_ref, state_ref, *refs):
    rows_refs, rows_hbm = refs[:4], refs[6:10]
    relation_hbm, state_hbm, relation_out, state_out, sems = *refs[4:6], *refs[10:13]
    nrel, width, _ = relation_ref.shape
    copies = [pltpu.make_async_copy(here, there, sems.at[i]) for i, (here, there) in enumerate(zip(rows_refs, rows_hbm))]
    for copy in copies:
        copy.start()
    for r in range(nrel):
        for part in range(2):
            cols = slice(part * 128, (part + 1) * 128)
            grad = total_ref[r, part].reshape(width, 128)
            state = state_ref[r, :, cols] + grad * grad
            state_out[r, :, cols] = state
            relation_out[r, :, cols] = relation_ref[r, :, cols] - learn_rate * grad / jnp.sqrt(state)
        for here, there in ((relation_out, relation_hbm), (state_out, state_hbm)):
            copies.append(pltpu.make_async_copy(here.at[r], there.at[r], sems.at[len(copies)]))
            copies[-1].start()
    for copy in copies:
        copy.wait()


def f32(*shape):
    return jax.ShapeDtypeStruct(shape, F32)


def call(kernel, name, outs, args, scratch=(), flops=0, outside=(), outputs_outside=False):
    out_space = pltpu.HBM if outputs_outside else pltpu.VMEM
    spaces = [pltpu.HBM if i in outside else pltpu.VMEM for i in range(len(args))]
    sems = [pltpu.SemaphoreType.DMA((len(outside),))] if outside else []
    return pl.pallas_call(
        kernel,
        out_shape=outs,
        in_specs=[pl.BlockSpec(memory_space=space) for space in spaces],
        out_specs=[pl.BlockSpec(memory_space=out_space)] * len(outs),
        scratch_shapes=[pltpu.VMEM(*one) if isinstance(one, tuple) else one for one in scratch] + sems,
        compiler_params=pltpu.CompilerParams(vmem_limit_bytes=30 << 20),
        cost_estimate=pl.CostEstimate(flops=flops, bytes_accessed=4 << 20, transcendentals=0),
        name=name,
    )(*(pltpu.with_memory_space_constraint(a, pltpu.HBM) if i in outside else a for i, a in enumerate(args)))


def buckets(index, left, left_accum, right, right_accum, relation, nbatch, move):
    nrel, width, _ = relation.shape
    rows = left.shape[0]
    pairs = nrel * rows
    half = rows // 2
    mine = NREL * half
    bf16 = lambda *shape: jax.ShapeDtypeStruct(shape, BF)
    counts = [((SLOTS, rows, mine), F32), ((SLOTS, 2, rows, LANES), F32)]
    moved, query_t, grad_bf, table_t = call(
        functools.partial(first_kernel, nbatch),
        "bucket0_left",
        (f32(half + 8, width), bf16(width, mine), bf16(rows, mine), bf16(width, mine)),
        (index, left, left_accum, right, relation),
        [((rows, mine), F32), *counts],
        flops=2 << 30,
    )
    moved = move(moved)
    right, right_accum, grad, edges, counts = call(
        functools.partial(between_kernel, nbatch),
        "bucket0_right",
        (f32(rows, width), f32(1, rows), f32(width, width), f32(SLOTS, rows, pairs), f32(SLOTS, 2, rows, LANES)),
        (index, left, right, right_accum, relation, query_t, grad_bf, table_t),
        [((width, mine), BF), ((rows, mine), F32), ((rows, mine), BF), *counts],
        flops=1 << 30,
    )
    moved = lax.all_gather(moved, "core", axis=0, tiled=False)
    return call(
        second_kernel,
        "bucket1",
        (f32(rows, width), f32(1, rows), f32(rows, width), f32(1, rows), f32(2, width // 4, 4, 128)),
        (edges, counts, moved, right, right_accum, relation, grad),
        [((width, pairs), BF), ((rows, pairs), F32), ((rows, pairs), BF), ((width, pairs), BF)],
        flops=2 << 30,
    )


def body(
    left_emb,
    left_state,
    right_emb,
    right_state,
    relation,
    relation_state,
    edge_src,
    edge_dst,
    edge_rel,
    negatives,
    batch_counts,
):
    nbatch, batch = edge_src.shape[3:]
    rows, width = left_emb.shape
    blocks = lax.axis_size(BLK)
    index_rows = -(-(8 * nbatch + 2) // 8) * 8
    arrays = (left_emb, left_state.reshape(1, rows), right_emb, right_state.reshape(1, rows), relation)
    index, *arrays = call(
        functools.partial(gather_kernel, nbatch),
        "gather_index",
        (jax.ShapeDtypeStruct((index_rows, batch), jnp.int32), *(f32(*array.shape) for array in arrays)),
        (edge_src, edge_dst, edge_rel, negatives, batch_counts, *arrays),
        [(edge_src.shape, jnp.int32)] * 4 + [pltpu.SMEM(batch_counts.shape, jnp.int32)],
        outside=tuple(range(10)),
    )
    index = lax.all_gather(index, REP, axis=0, tiled=False)
    route = [(i, (i + 1) % blocks) for i in range(blocks)]
    left, left_accum, right, right_accum, grad = buckets(
        index,
        *arrays,
        nbatch,
        lambda half: lax.ppermute(half, BLK, route),
    )
    grad = grad.reshape(blocks, -1, 128)
    grad = jnp.sum(lax.all_to_all(grad, BLK, 0, 0, tiled=True), axis=0)
    grad = jnp.broadcast_to(grad[None], (blocks, *grad.shape))
    grad = lax.all_to_all(grad, BLK, 0, 0, tiled=True)
    grad = lax.all_gather(grad, "core", axis=0, tiled=False)
    grad = grad.reshape(relation.shape[0], 2, width // 4, 4, 128)
    updated = (left, left_accum, right, right_accum)
    relation_new, relation_state_new, left, left_accum, right, right_accum = call(
        final_kernel,
        "final_update",
        tuple(f32(*array.shape) for array in (relation, relation_state, *updated)),
        (grad, arrays[-1], relation_state, *updated),
        [(relation.shape, F32)] * 2 + [pltpu.SemaphoreType.DMA((8,))],
        outputs_outside=True,
    )
    return (
        left,
        left_accum.reshape(rows),
        right,
        right_accum.reshape(rows),
        relation_new,
        relation_state_new,
    )


def solution(mesh):
    sizes = (8, 8, 2, 2, 2)
    mesh = jax.sharding.Mesh(mesh.devices.reshape(sizes), (*BLK, *REP))
    row, edge = P(BLK, None), P(BLK, REP, None, None, None)
    in_specs = (row, P(BLK), row, P(BLK), P(), P(), edge, edge, edge, edge, P(BLK, REP, None))
    out_specs = (row, P(BLK), row, P(BLK), P(), P())
    return jax.shard_map(body, mesh=mesh, in_specs=in_specs, out_specs=out_specs, check_vma=False)
```
